512 devices in a mesh: rows: 64 (over x, z), cols: 8 (over y, core).
Axes of the slice: x: 4, y: 4, z: 16, core: 2. Of those that a mesh axis runs over, the one named last changes fastest.
Arguments:
- features: float32 [16, 32768], P(None, ('rows', 'cols')), may hold values from -4 to 4
- targets: float32 [32, 32768], P(None, ('rows', 'cols')), may hold values from -6 to 6
- point_order: int32 [32768], P(('rows', 'cols')), may hold values from 0 to 32767, as said below
- lengthscale: float32 [16], replicated, may hold values from 1 to 1.8
- noise_var: float32 [32], replicated, may hold values from 0.1 to 1
Outputs:
- solution: float32 [32, 32768], P(None, ('rows', 'cols'))
- residual: float32 [32, 32768], P(None, ('rows', 'cols'))
The draws below stay inside these ranges and needn't reach their ends.
Inputs may be any that keep to these rules, and one draw needn't show every extreme that they name: `point_order`: each aligned block of 512 entries, the k-th one, holds each of the numbers k * 512 to k * 512 + 511 exactly once.
All inputs are finite; a program needn't handle non-finite values.
Results may differ from the reference program's by a relative error of at most 0.0051.
Values may be sent and summed in bfloat16 or wider, within the bound.
No kernel may reach another device: no remote copies, remote signals or barrier semaphores. Data moves between devices by JAX's collectives and lax.ppermute only.
A program may use at most 64 MiB of HBM per device.

```python
import math
import jax
import jax.numpy as jnp
from jax import lax

FEATS = 16
RHS = 32
INNER = 3
OUTER = 2
BLOCK = 512
POINTS = 32768
N_ROWS = 64


def draw_point_order(key, part):
    blocks = POINTS // BLOCK
    keys = jax.random.split(jax.random.fold_in(key, 7), blocks)
    shuffled = jax.vmap(lambda subkey: jax.random.permutation(subkey, BLOCK))(keys)
    offsets = jnp.arange(blocks, dtype=jnp.int32) * BLOCK
    return (shuffled.astype(jnp.int32) + offsets[:, None]).reshape(POINTS)


def draw_features(key, part):
    subkey = jax.random.fold_in(key, 11)
    return jnp.clip(jax.random.normal(subkey, (FEATS, POINTS), jnp.float32), -4.0, 4.0)


def steps_of(rng, extent, cuts, least, high):
    factor_of, own = 1.0, jax.random.fold_in(rng, 6)
    for position, shards_of in cuts:
        steps = jnp.exp(jax.random.uniform(jax.random.fold_in(own, position), (shards_of,), jnp.float32, least / len(cuts), high / len(cuts)))
        factor_of = factor_of * jnp.repeat(steps, extent[position] // shards_of).reshape([-1 if axis == position else 1 for axis in range(len(extent))])
    return factor_of


def scatter_about(key, extent, scale, limit, cuts=(), kind=jnp.bfloat16):
    factor_of = steps_of(key, extent, cuts, -0.22, 0.18) if cuts else 1.0
    array = jax.random.normal(key, extent, jnp.float32) * scale * factor_of
    return jnp.minimum(jnp.maximum(array, -limit), limit).astype(kind)


def setup_inputs(seed: int = 0) -> dict:
    seeds = jax.random.split(jax.random.key(seed), 6)
    features = draw_features(jax.random.fold_in(seeds[5], 71), 0)
    targets = scatter_about(seeds[1], (RHS, POINTS), 1.0, 6.0, ((1, 512),), jnp.float32)
    point_order = draw_point_order(jax.random.fold_in(seeds[5], 71), 0)
    lengthscale = jnp.clip(jnp.exp(jax.random.uniform(seeds[3], (FEATS,), jnp.float32, math.log(1.0), math.log(1.8))), 1.0, 1.8)
    noise_var = jnp.clip(jnp.exp(jax.random.uniform(seeds[4], (RHS,), jnp.float32, math.log(0.1), math.log(1.0))), 0.1, 1.0)
    return dict(features=features, targets=targets, point_order=point_order, lengthscale=lengthscale, noise_var=noise_var)


def kernel_tile(col_feat, col_norm, row_feat, row_norm):
    inner_prod = jnp.dot(col_feat.T, row_feat, precision=lax.Precision.HIGHEST, preferred_element_type=jnp.float32)
    return jnp.exp(-0.5 * (col_norm[:, None] + row_norm[None, :] - 2.0 * inner_prod)).astype(jnp.bfloat16)


def apply_full(vectors, scaled, norms, noise_var):
    packed = lax.optimization_barrier(vectors.astype(jnp.bfloat16)).astype(jnp.float32)
    points = scaled.shape[1]
    span_rows = math.gcd(points, 512)

    def one_block(which):
        row_feat = lax.dynamic_slice_in_dim(scaled, which * span_rows, span_rows, 1)
        row_norm = lax.dynamic_slice_in_dim(norms, which * span_rows, span_rows, 0)
        kern_tile = lax.optimization_barrier(kernel_tile(scaled, norms, row_feat, row_norm)).astype(jnp.float32)
        return jnp.dot(packed, kern_tile, precision=lax.Precision.HIGHEST, preferred_element_type=jnp.float32)

    result = lax.map(one_block, jnp.arange(points // span_rows, dtype=jnp.int32))
    result = jnp.transpose(result, (1, 0, 2)).reshape(vectors.shape)
    return result + noise_var[:, None] * vectors


def block_kernels(scaled, norms):
    blocked = scaled.reshape(FEATS, N_ROWS, BLOCK).transpose(1, 0, 2)
    block_norms = norms.reshape(N_ROWS, BLOCK)

    def single(pair):
        return kernel_tile(pair[0], pair[1], pair[0], pair[1])

    return lax.map(single, (blocked, block_norms))


def block_solve(residual, kernels, noise_var):
    kern_wide = kernels.astype(jnp.float32)
    rhs_blocks = residual.reshape(RHS, N_ROWS, BLOCK)
    res_norm = jnp.sum(rhs_blocks * rhs_blocks, 2)
    direction = rhs_blocks
    correction = jnp.zeros_like(rhs_blocks)
    for inner_turn in range(INNER):
        packed = lax.optimization_barrier(direction.astype(jnp.bfloat16)).astype(jnp.float32)
        applied = jnp.einsum("rbj,bji->rbi", packed, kern_wide, precision=lax.Precision.HIGHEST)
        applied = applied + noise_var[:, None, None] * direction
        curvature = jnp.sum(direction * applied, 2)
        step_len = res_norm / curvature
        correction = correction + step_len[:, :, None] * direction
        rhs_blocks = rhs_blocks - step_len[:, :, None] * applied
        if inner_turn + 1 < INNER:
            new_norm = jnp.sum(rhs_blocks * rhs_blocks, 2)
            direction = rhs_blocks + (new_norm / res_norm)[:, :, None] * direction
            res_norm = new_norm
    return correction.reshape(RHS, N_ROWS * BLOCK)


def reference(features, targets, point_order, lengthscale, noise_var):
    scaled = features / lengthscale[:, None]
    norms = jnp.sum(scaled * scaled, 0)
    residual = jnp.take(targets, point_order, axis=1)
    kernels = block_kernels(scaled, norms)
    solution = jnp.zeros_like(residual)
    for outer_turn in range(OUTER):
        correction = block_solve(residual, kernels, noise_var)
        applied = apply_full(correction, scaled, norms, noise_var)
        cross_term = jnp.sum(residual * applied, 1)
        energy = jnp.sum(applied * applied, 1)
        damping_w = cross_term / (energy + 1e-6)
        solution = solution + damping_w[:, None] * correction
        residual = residual - damping_w[:, None] * applied
    return solution, residual
```

```python
import jax
import jax.numpy as jnp
from jax import lax
from jax.experimental import pallas as pl
from jax.experimental.pallas import tpu as pltpu
from jax.sharding import Mesh
from jax.sharding import PartitionSpec as P

INNER = 3
X, Z, Y, K = "rows_0", "rows_1", "cols_0", "cols_1"
ROWS, COLS, PLANE = (X, Z), (Y, K), (X, Y, K)
ROWS_COLS = (X, Z, Y, K)
N_X, N_Z, N_C = 4, 16, 8
FEATS, RHS, OWN, BLOCK = 16, 32, 64, 512
LINE, FLAT = N_Z * OWN, N_X * BLOCK
DEPTH = 7 * FEATS
ROOT_LOG2E = 1.4426950408889634**0.5
F32, BF16 = jnp.float32, jnp.bfloat16
PARAMS = pltpu.CompilerParams(vmem_limit_bytes=40 * 1024 * 1024)


def low_lanes(rows):
    return lax.broadcasted_iota(jnp.int32, (rows, 2 * OWN), 1) < OWN


def join(a, b):
    low = low_lanes(a.shape[0])
    top = jnp.where(low, a, pltpu.roll(b, OWN, 1))
    bottom = jnp.where(low, pltpu.roll(a, OWN, 1), b)
    return jnp.concatenate([top, bottom], axis=0)


def part(field):
    half = field.shape[0] // 2
    top, bottom = field[:half], field[half:]
    low = low_lanes(half)
    return (
        jnp.where(low, top, pltpu.roll(bottom, OWN, 1)),
        jnp.where(low, pltpu.roll(top, OWN, 1), bottom),
    )


def join_all(pieces):
    tiles = [join(a, b) for a, b in zip(pieces[0::2], pieces[1::2])]
    return jnp.concatenate(tiles, axis=1)


def part_all(field):
    pieces = []
    for at in range(0, field.shape[1], 2 * OWN):
        pieces += part(field[:, at : at + 2 * OWN])
    return pieces


def own_piece(pieces):
    me = lax.axis_index(COLS)
    mine = jnp.zeros_like(pieces[0])
    for which, piece in enumerate(pieces):
        mine = jnp.where(me == which, piece, mine)
    return mine


def by_half(column):
    half = column.shape[0] // 2
    return jnp.where(low_lanes(half), column[:half], column[half:])


def three(value):
    first = value.astype(BF16).astype(F32)
    second = (value - first).astype(BF16).astype(F32)
    third = (value - first - second).astype(BF16).astype(F32)
    return first, second, third


def factors(parts, side):
    p1, p2, p3 = parts
    scaled = p1 + (p2 + p3)
    h1, h2, h3 = three(-0.5 * jnp.sum(scaled * scaled, axis=0, keepdims=True))
    row = lax.broadcasted_iota(jnp.int32, scaled.shape, 0)
    at = 0 if side == 0 else 3
    tail = jnp.where(row < 6, 1.0, 0.0)
    for offset, h in enumerate((h1, h2, h3)):
        tail = jnp.where(row == at + offset, h, tail)
    order = (p1, p1, p2, p2, p1, p3) if side == 0 else (p1, p2, p1, p2, p3, p1)
    return jnp.concatenate([*order, tail], axis=0).astype(BF16)


def kernel_of(left, right):
    exponent = lax.dot_general(
        left, right, (((0,), (0,)), ((), ())), preferred_element_type=F32
    )
    return jnp.exp2(exponent).astype(BF16)


def block_cg(residual, kern, noise):
    remains, direction = residual, residual
    correction = jnp.zeros_like(residual)
    res_norm = jnp.sum(remains * remains, axis=1, keepdims=True)
    for turn in range(INNER):
        image = jnp.dot(direction.astype(BF16), kern, preferred_element_type=F32)
        image = image + noise * direction
        step = res_norm / jnp.sum(direction * image, axis=1, keepdims=True)
        correction = correction + step * direction
        remains = remains - step * image
        if turn + 1 < INNER:
            new_norm = jnp.sum(remains * remains, axis=1, keepdims=True)
            direction = remains + (new_norm / res_norm) * direction
            res_norm = new_norm
    return correction


def sums_row(residual, applied):
    lane = lax.broadcasted_iota(jnp.int32, (RHS, 128), 1)
    cross = jnp.sum(residual * applied, axis=1, keepdims=True)
    energy = jnp.sum(applied * applied, axis=1, keepdims=True)
    turned = jnp.where(lane == 0, cross, jnp.where(lane == 1, energy, 0.0)).T
    blank = jnp.zeros((1, 128 - 2 * RHS), F32)
    return jnp.concatenate([turned[0:1], turned[1:2], blank], axis=1)


def damping_of(rows):
    total = jnp.sum(rows, axis=0, keepdims=True)
    turned = jnp.broadcast_to(total, (8, 128)).T
    return turned[0:RHS, 0:1] / (turned[RHS : 2 * RHS, 0:1] + 1e-6)


def pack_body(feat_ref, targ_ref, order_ref, scale_ref, cols_ref, plane_ref):
    def halves(field):
        half = field.shape[0] // 2
        return jnp.concatenate([field[:half], field[half:]], axis=1)

    scaled = halves(feat_ref[...] / scale_ref[...] * ROOT_LOG2E)
    order = (order_ref[...] % BLOCK).astype(F32)
    order = jnp.concatenate([order, order], axis=1)
    order = jnp.broadcast_to(order, (8, 2 * OWN))
    whole = jnp.concatenate([scaled, halves(targ_ref[...]), order], axis=0)
    for to in range(N_C):
        cols_ref[to] = whole
    for to in range(N_X * N_C):
        plane_ref[to] = scaled


def first_body(recv_ref, noise_ref, msg_ref, kern_ref, res_ref, corr_ref):
    pieces = [recv_ref[i] for i in range(N_C)]
    parts = three(join_all([p[0:8] for p in pieces]))
    kern = kernel_of(factors(parts, 0), factors(parts, 1))
    kern_ref[...] = kern
    low = low_lanes(1)
    order = [
        jnp.where(low, a[24:25], b[24:25]) for a, b in zip(pieces[0::2], pieces[1::2])
    ]
    order = jnp.concatenate(order, axis=1).astype(jnp.int32)
    index = lax.broadcasted_iota(jnp.int32, (BLOCK, BLOCK), 0)
    pick = jnp.where(index == order, 1.0, 0.0).astype(BF16)
    targets = three(join_all([p[8:24] for p in pieces]))
    stack = jnp.concatenate(targets, axis=0).astype(BF16)
    moved = jnp.dot(stack, pick, preferred_element_type=F32)
    residual = moved[0:RHS] + (moved[RHS : 2 * RHS] + moved[2 * RHS :])
    res_ref[...] = residual
    correction = own_piece(part_all(block_cg(residual, kern, noise_ref[...])))
    corr_ref[...] = correction
    mine = three(own_piece([p[0:8] for p in pieces]))
    whole = jnp.concatenate([*mine, correction], axis=0).astype(BF16)
    for to in range(N_Z):
        msg_ref[to] = whole


def spread(msg_ref, at, field):
    for which, piece in enumerate(part_all(field)):
        msg_ref[at + which] = piece


TILE = 256


def build_body(line_ref, plane_ref, msg_ref, kern_ref, left_ref, right_ref):
    line = [line_ref[i].astype(F32) for i in range(N_Z)]
    for p in range(N_Z // 2):
        a, b = line[2 * p], line[2 * p + 1]
        parts = [join(a[i : i + 8], b[i : i + 8]) for i in (0, 8, 16)]
        left_ref[:, pl.ds(128 * p, 128)] = factors(parts, 0)
    for p in range(N_X * N_C // 2):
        parts = three(join(plane_ref[2 * p], plane_ref[2 * p + 1]))
        right_ref[:, pl.ds(128 * p, 128)] = factors(parts, 1)
    corr = join_all([piece[24:40] for piece in line]).astype(BF16)

    def step(i, carry):
        at = pl.multiple_of(i * TILE, TILE)
        kern = kernel_of(left_ref[...], right_ref[:, pl.ds(at, TILE)])
        kern_ref[:, pl.ds(at, TILE)] = kern
        field = jnp.dot(corr, kern, preferred_element_type=F32)
        spread(msg_ref, i * (TILE // OWN), field)
        return carry

    lax.fori_loop(0, FLAT // TILE, step, 0)


def again_body(line_ref, kern_ref, msg_ref):
    corr = join_all([line_ref[i].astype(F32) for i in range(N_Z)]).astype(BF16)

    def step(i, carry):
        at = pl.multiple_of(i * TILE, TILE)
        field = jnp.dot(corr, kern_ref[:, pl.ds(at, TILE)], preferred_element_type=F32)
        spread(msg_ref, i * (TILE // OWN), field)
        return carry

    lax.fori_loop(0, FLAT // TILE, step, 0)


def applied_of(recv_ref, corr_ref, noise_ref):
    total = recv_ref[0]
    for i in range(1, N_X * N_C):
        total = total + recv_ref[i]
    return total + by_half(noise_ref[...]) * corr_ref[...]


def share_body(recv_ref, corr_ref, noise_ref, msg_ref):
    applied = applied_of(recv_ref, corr_ref, noise_ref)
    for to in range(N_C):
        msg_ref[to] = applied


def sums_body(recv_ref, res_ref, msg_ref):
    applied = join_all([recv_ref[i] for i in range(N_C)])
    row = sums_row(res_ref[...], applied)
    msg_ref[...] = jnp.broadcast_to(row, msg_ref.shape)


def second_body(
    rows_ref, recv_ref, res_ref, corr_ref, kern_ref, noise_ref, msg_ref, new_ref, sol_ref, mine_ref
):
    damping = damping_of(rows_ref[...])
    applied = join_all([recv_ref[i] for i in range(N_C)])
    residual = res_ref[...] - damping * applied
    sol_ref[...] = by_half(damping) * corr_ref[...]
    mine_ref[...] = own_piece(part_all(residual))
    correction = own_piece(part_all(block_cg(residual, kern_ref[...], noise_ref[...])))
    new_ref[...] = correction
    whole = correction.astype(BF16)
    for to in range(N_Z):
        msg_ref[to] = whole


def last_sums_body(recv_ref, corr_ref, noise_ref, mine_ref, msg_ref, applied_ref):
    applied = applied_of(recv_ref, corr_ref, noise_ref)
    applied_ref[...] = applied
    row = sums_row(split_halves(mine_ref[...]), split_halves(applied))
    msg_ref[...] = jnp.broadcast_to(row, msg_ref.shape)


def split_halves(field):
    return jnp.concatenate([field[:, :OWN], field[:, OWN:]], axis=0)


def gather_body(recv_ref, msg_ref):
    total = jnp.sum(recv_ref[...], axis=0, keepdims=True)
    msg_ref[...] = jnp.broadcast_to(total, msg_ref.shape)


def end_body(rows_ref, applied_ref, corr_ref, sol_ref, mine_ref, sol_out, res_out):
    damping = by_half(damping_of(rows_ref[...]))
    sol_out[...] = split_halves(sol_ref[...] + damping * corr_ref[...])
    res_out[...] = split_halves(mine_ref[...] - damping * applied_ref[...])


def call(body, outs, *args, scratch=(), name):
    return pl.pallas_call(
        body,
        out_shape=[jax.ShapeDtypeStruct(s, d) for s, d in outs],
        in_specs=[pl.BlockSpec(memory_space=pltpu.VMEM)] * len(args),
        out_specs=[pl.BlockSpec(memory_space=pltpu.VMEM)] * len(outs),
        scratch_shapes=list(scratch),
        compiler_params=PARAMS,
        name=name,
    )(*args)


def swap(array, axis):
    return lax.all_to_all(array, axis, split_axis=0, concat_axis=0, tiled=True)


def body(features, targets, point_order, lengthscale, noise_var):
    noise = noise_var[:, None]
    packed = (OWN // 4, 2 * OWN)
    cols_msg, plane_msg = call(
        pack_body,
        [((N_C, 32, 128), F32), ((N_X * N_C, 8, 128), F32)],
        features,
        targets,
        point_order[None, :],
        lengthscale[:, None],
        name="pack",
    )
    block = swap(cols_msg, COLS)
    plane = swap(plane_msg, PLANE)
    line_msg, kern_b, res, corr = call(
        first_body,
        [
            ((N_Z, 40, 128), BF16),
            ((BLOCK, BLOCK), BF16),
            ((RHS, BLOCK), F32),
            (packed, F32),
        ],
        block,
        noise,
        name="first",
    )
    line = swap(line_msg, Z)
    flat_msg, kern = call(
        build_body,
        [((N_X * N_C, *packed), F32), ((LINE, FLAT), BF16)],
        line,
        plane,
        scratch=[pltpu.VMEM((DEPTH, LINE), BF16), pltpu.VMEM((DEPTH, FLAT), BF16)],
        name="build",
    )
    flat = swap(flat_msg, PLANE)
    (share_msg,) = call(
        share_body, [((N_C, *packed), F32)], flat, corr, noise, name="share"
    )
    shared = swap(share_msg, COLS)
    (sums_msg,) = call(sums_body, [((N_X * N_Z, 128), F32)], shared, res, name="sums")
    sums = swap(sums_msg, ROWS)
    line_msg, corr_2, sol, mine = call(
        second_body,
        [((N_Z, *packed), BF16), (packed, F32), (packed, F32), (packed, F32)],
        sums,
        shared,
        res,
        corr,
        kern_b,
        noise,
        name="second",
    )
    line = swap(line_msg, Z)
    (flat_msg,) = call(
        again_body, [((N_X * N_C, *packed), F32)], line, kern, name="again"
    )
    flat = swap(flat_msg, PLANE)
    near_msg, applied = call(
        last_sums_body,
        [((N_C, 128), F32), (packed, F32)],
        flat,
        corr_2,
        noise,
        mine,
        name="last_sums",
    )
    near = swap(near_msg, COLS)
    (sums_msg,) = call(gather_body, [((N_X * N_Z, 128), F32)], near, name="near")
    sums = swap(sums_msg, ROWS)
    return tuple(
        call(
            end_body,
            [((RHS, OWN), F32)] * 2,
            sums,
            applied,
            corr_2,
            sol,
            mine,
            name="end",
        )
    )


def solution(mesh):
    finer = Mesh(mesh.devices.reshape(N_X, N_Z, 4, 2), ROWS_COLS)
    in_specs = (P(None, ROWS_COLS), P(None, ROWS_COLS), P(ROWS_COLS), P(), P())
    out_specs = (P(None, ROWS_COLS), P(None, ROWS_COLS))
    return jax.shard_map(body, mesh=finer, in_specs=in_specs, out_specs=out_specs, check_vma=False)
```

```python
import jax
import jax.numpy as jnp
from jax import lax
from jax.experimental import pallas as pl
from jax.experimental.pallas import tpu as pltpu
from jax.sharding import Mesh
from jax.sharding import PartitionSpec as P

INNER = 3
X, Z, Y, K = "rows_0", "rows_1", "cols_0", "cols_1"
ROWS, COLS, PLANE = (X, Z), (Y, K), (X, Y, K)
ROWS_COLS = (X, Z, Y, K)
N_X, N_Z, N_C = 4, 16, 8
FEATS, RHS, OWN, BLOCK = 16, 32, 64, 512
LINE, FLAT = N_Z * OWN, N_X * BLOCK
DEPTH = 7 * FEATS
ROOT_LOG2E = 1.4426950408889634**0.5
F32, BF16 = jnp.float32, jnp.bfloat16
PARAMS = pltpu.CompilerParams(vmem_limit_bytes=12 * 1024 * 1024)


def low_lanes(rows):
    return lax.broadcasted_iota(jnp.int32, (rows, 2 * OWN), 1) < OWN


def join(a, b):
    low = low_lanes(a.shape[0])
    top = jnp.where(low, a, pltpu.roll(b, OWN, 1))
    bottom = jnp.where(low, pltpu.roll(a, OWN, 1), b)
    return jnp.concatenate([top, bottom], axis=0)


def part(field):
    half = field.shape[0] // 2
    top, bottom = field[:half], field[half:]
    low = low_lanes(half)
    return (
        jnp.where(low, top, pltpu.roll(bottom, OWN, 1)),
        jnp.where(low, pltpu.roll(top, OWN, 1), bottom),
    )


def join_all(pieces):
    tiles = [join(a, b) for a, b in zip(pieces[0::2], pieces[1::2])]
    return jnp.concatenate(tiles, axis=1)


def part_all(field):
    pieces = []
    for at in range(0, field.shape[1], 2 * OWN):
        pieces += part(field[:, at : at + 2 * OWN])
    return pieces


def own_piece(pieces):
    me = lax.axis_index(COLS)
    mine = jnp.zeros_like(pieces[0])
    for which, piece in enumerate(pieces):
        mine = jnp.where(me == which, piece, mine)
    return mine


def by_half(column):
    half = column.shape[0] // 2
    return jnp.where(low_lanes(half), column[:half], column[half:])


def three(value):
    first = value.astype(BF16).astype(F32)
    second = (value - first).astype(BF16).astype(F32)
    third = (value - first - second).astype(BF16).astype(F32)
    return first, second, third


def factors(parts, side):
    p1, p2, p3 = parts
    scaled = p1 + (p2 + p3)
    h1, h2, h3 = three(-0.5 * jnp.sum(scaled * scaled, axis=0, keepdims=True))
    row = lax.broadcasted_iota(jnp.int32, scaled.shape, 0)
    at = 0 if side == 0 else 3
    tail = jnp.where(row < 6, 1.0, 0.0)
    for offset, h in enumerate((h1, h2, h3)):
        tail = jnp.where(row == at + offset, h, tail)
    order = (p1, p1, p2, p2, p1, p3) if side == 0 else (p1, p2, p1, p2, p3, p1)
    return jnp.concatenate([*order, tail], axis=0).astype(BF16)


def kernel_of(left, right):
    exponent = lax.dot_general(
        left, right, (((0,), (0,)), ((), ())), preferred_element_type=F32
    )
    return jnp.exp2(exponent).astype(BF16)


def block_cg(residual, kern, noise):
    remains, direction = residual, residual
    correction = jnp.zeros_like(residual)
    res_norm = jnp.sum(remains * remains, axis=1, keepdims=True)
    for turn in range(INNER):
        image = jnp.dot(direction.astype(BF16), kern, preferred_element_type=F32)
        image = image + noise * direction
        step = res_norm / jnp.sum(direction * image, axis=1, keepdims=True)
        correction = correction + step * direction
        remains = remains - step * image
        if turn + 1 < INNER:
            new_norm = jnp.sum(remains * remains, axis=1, keepdims=True)
            direction = remains + (new_norm / res_norm) * direction
            res_norm = new_norm
    return correction


def sums_row(residual, applied):
    lane = lax.broadcasted_iota(jnp.int32, (RHS, 128), 1)
    cross = jnp.sum(residual * applied, axis=1, keepdims=True)
    energy = jnp.sum(applied * applied, axis=1, keepdims=True)
    turned = jnp.where(lane == 0, cross, jnp.where(lane == 1, energy, 0.0)).T
    blank = jnp.zeros((1, 128 - 2 * RHS), F32)
    return jnp.concatenate([turned[0:1], turned[1:2], blank], axis=1)


def damping_of(rows):
    total = jnp.sum(rows, axis=0, keepdims=True)
    turned = jnp.broadcast_to(total, (8, 128)).T
    return turned[0:RHS, 0:1] / (turned[RHS : 2 * RHS, 0:1] + 1e-6)


def pack_body(
    feat_any, targ_any, order_any, scale_any, noise_any,
    plane_ref, noise_ref,
    feat_ref, targ_ref, order_ref, scale_ref, given_ref, sems,
):
    pairs = (
        (scale_any, scale_ref),
        (noise_any, given_ref),
        (feat_any, feat_ref),
        (targ_any, targ_ref),
        (order_any, order_ref),
    )
    copies = [
        pltpu.make_async_copy(src, dst, sems.at[i]) for i, (src, dst) in enumerate(pairs)
    ]
    for copy in copies:
        copy.start()
    for copy in copies:
        copy.wait()

    def halves(field):
        half = field.shape[0] // 2
        return jnp.concatenate([field[:half], field[half:]], axis=1)

    def column(source, shape):
        row = lax.broadcasted_iota(jnp.int32, shape, 0)
        filled = jnp.zeros(shape, F32)
        for i in range(shape[0]):
            filled = jnp.where(row == i, source[i], filled)
        return filled

    scaled = halves(feat_ref[...] / column(scale_ref, (FEATS, OWN)) * ROOT_LOG2E)
    order = (order_ref[...] % BLOCK).astype(F32)
    order = jnp.concatenate([order, order], axis=1)
    order = jnp.broadcast_to(order, (8, 2 * OWN))
    whole = jnp.concatenate([scaled, halves(targ_ref[...]), order], axis=0)
    for to in range(N_X * N_C):
        plane_ref[to] = whole
    noise_ref[...] = column(given_ref, (RHS, 128))


def first_body(recv_ref, noise_ref, msg_ref, kern_ref, res_ref, corr_ref):
    base = lax.axis_index(X) * N_C
    pieces = [recv_ref[base + i] for i in range(N_C)]
    parts = three(join_all([p[0:8] for p in pieces]))
    kern = kernel_of(factors(parts, 0), factors(parts, 1))
    kern_ref[...] = kern
    low = low_lanes(1)
    order = [
        jnp.where(low, a[24:25], b[24:25]) for a, b in zip(pieces[0::2], pieces[1::2])
    ]
    order = jnp.concatenate(order, axis=1).astype(jnp.int32)
    index = lax.broadcasted_iota(jnp.int32, (BLOCK, BLOCK), 0)
    pick = jnp.where(index == order, 1.0, 0.0).astype(BF16)
    targets = three(join_all([p[8:24] for p in pieces]))
    stack = jnp.concatenate(targets, axis=0).astype(BF16)
    moved = jnp.dot(stack, pick, preferred_element_type=F32)
    residual = moved[0:RHS] + (moved[RHS : 2 * RHS] + moved[2 * RHS :])
    res_ref[...] = residual
    correction = own_piece(part_all(block_cg(residual, kern, noise_ref[:, 0:1])))
    corr_ref[...] = correction
    mine = three(own_piece([p[0:8] for p in pieces]))
    whole = jnp.concatenate([*mine, correction], axis=0).astype(BF16)
    for to in range(N_Z):
        msg_ref[to] = whole


def spread(msg_ref, at, field):
    for which, piece in enumerate(part_all(field)):
        msg_ref[at + which] = piece


TILE = 256
STEP = min(LINE, 256)


def build_body(line_ref, plane_ref, msg_ref, kern_ref, left_ref, right_ref):
    line = [line_ref[i].astype(F32) for i in range(N_Z)]
    for p in range(N_Z // 2):
        a, b = line[2 * p], line[2 * p + 1]
        parts = [join(a[i : i + 8], b[i : i + 8]) for i in (0, 8, 16)]
        left_ref[:, pl.ds(128 * p, 128)] = factors(parts, 0)
    for p in range(N_X * N_C // 2):
        parts = three(join(plane_ref[2 * p, 0:8], plane_ref[2 * p + 1, 0:8]))
        right_ref[:, pl.ds(128 * p, 128)] = factors(parts, 1)
    corr = join_all([piece[24:40] for piece in line]).astype(BF16)

    def step(i, carry):
        at = pl.multiple_of(i * TILE, TILE)
        kern = kernel_of(left_ref[...], right_ref[:, pl.ds(at, TILE)])
        kern_ref[:, pl.ds(at, TILE)] = kern
        field = jnp.dot(corr, kern, preferred_element_type=F32)
        spread(msg_ref, i * (TILE // OWN), field)
        return carry

    lax.fori_loop(0, FLAT // TILE, step, 0)


def apply_body(flat_ref, kern_ref, msg_ref):
    corr = jnp.concatenate([flat_ref[i].astype(F32) for i in range(N_X)], axis=1)
    turned = corr.T.astype(BF16)

    def step(i, carry):
        at = pl.multiple_of(i * STEP, STEP)
        field = jnp.dot(
            kern_ref[pl.ds(at, STEP), :], turned, preferred_element_type=F32
        )
        spread(msg_ref, i * (STEP // OWN), field.T)
        return carry

    lax.fori_loop(0, LINE // STEP, step, 0)


def applied_of(recv_ref, corr_ref, noise_ref):
    total = recv_ref[0]
    for i in range(1, recv_ref.shape[0]):
        total = total + recv_ref[i]
    return total + by_half(noise_ref[:, 0:1]) * corr_ref[...]


def share_body(recv_ref, corr_ref, noise_ref, msg_ref):
    applied = applied_of(recv_ref, corr_ref, noise_ref)
    for to in range(N_C):
        msg_ref[to] = applied


def sums_body(recv_ref, res_ref, msg_ref):
    applied = join_all([recv_ref[i] for i in range(N_C)])
    row = sums_row(res_ref[...], applied)
    msg_ref[...] = jnp.broadcast_to(row, msg_ref.shape)


def second_body(
    rows_ref, recv_ref, res_ref, corr_ref, kern_ref, noise_ref, msg_ref, new_ref, sol_ref, mine_ref
):
    damping = damping_of(rows_ref[...])
    applied = join_all([recv_ref[i] for i in range(N_C)])
    residual = res_ref[...] - damping * applied
    sol_ref[...] = by_half(damping) * corr_ref[...]
    mine_ref[...] = own_piece(part_all(residual))
    correction = block_cg(residual, kern_ref[...], noise_ref[:, 0:1])
    new_ref[...] = own_piece(part_all(correction))
    whole = correction.astype(BF16)
    for to in range(N_X):
        msg_ref[to] = whole


def last_sums_body(recv_ref, corr_ref, noise_ref, mine_ref, msg_ref, applied_ref):
    applied = applied_of(recv_ref, corr_ref, noise_ref)
    applied_ref[...] = applied
    row = sums_row(split_halves(mine_ref[...]), split_halves(applied))
    msg_ref[...] = jnp.broadcast_to(row, msg_ref.shape)


def split_halves(field):
    return jnp.concatenate([field[:, :OWN], field[:, OWN:]], axis=0)


def gather_body(recv_ref, msg_ref):
    total = jnp.sum(recv_ref[...], axis=0, keepdims=True)
    msg_ref[...] = jnp.broadcast_to(total, msg_ref.shape)


def end_body(rows_ref, applied_ref, corr_ref, sol_ref, mine_ref, sol_out, res_out):
    damping = by_half(damping_of(rows_ref[...]))
    sol_out[...] = split_halves(sol_ref[...] + damping * corr_ref[...])
    res_out[...] = split_halves(mine_ref[...] - damping * applied_ref[...])


def call(body, outs, *args, scratch=(), space=pltpu.VMEM, flops=1 << 20, name):
    return pl.pallas_call(
        body,
        out_shape=[jax.ShapeDtypeStruct(s, d) for s, d in outs],
        in_specs=[pl.BlockSpec(memory_space=space)] * len(args),
        out_specs=[pl.BlockSpec(memory_space=pltpu.VMEM)] * len(outs),
        scratch_shapes=list(scratch),
        compiler_params=PARAMS,
        cost_estimate=pl.CostEstimate(flops=flops, transcendentals=0, bytes_accessed=1 << 20),
        name=name,
    )(*args)


def stay(array):
    return pltpu.with_memory_space_constraint(array, pltpu.HBM)


def swap(array, axis):
    return lax.all_to_all(array, axis, split_axis=0, concat_axis=0, tiled=True)


def body(features, targets, point_order, lengthscale, noise_var):
    packed = (RHS // 2, 2 * OWN)
    n_p = N_X * N_C
    plane_msg, noise = call(
        pack_body,
        [((n_p, 32, 128), F32), ((RHS, 128), F32)],
        *map(stay, (features, targets, point_order[None, :], lengthscale, noise_var)),
        scratch=[
            pltpu.VMEM((FEATS, OWN), F32),
            pltpu.VMEM((RHS, OWN), F32),
            pltpu.VMEM((1, OWN), jnp.int32),
            pltpu.SMEM((FEATS,), F32),
            pltpu.SMEM((RHS,), F32),
            pltpu.SemaphoreType.DMA((5,)),
        ],
        space=pltpu.HBM,
        name="pack",
    )
    plane = swap(plane_msg, PLANE)
    line_msg, kern_b, res, corr = call(
        first_body,
        [
            ((N_Z, 40, 128), BF16),
            ((BLOCK, BLOCK), BF16),
            ((RHS, BLOCK), F32),
            (packed, F32),
        ],
        plane,
        noise,
        name="first",
    )
    line = swap(line_msg, Z)
    flat_msg, kern = call(
        build_body,
        [((n_p, *packed), F32), ((LINE, FLAT), BF16)],
        line,
        plane,
        scratch=[pltpu.VMEM((DEPTH, LINE), BF16), pltpu.VMEM((DEPTH, FLAT), BF16)],
        name="build",
    )
    flat = swap(flat_msg, PLANE)
    (share_msg,) = call(
        share_body, [((N_C, *packed), F32)], flat, corr, noise, name="share"
    )
    shared = swap(share_msg, COLS)
    (sums_msg,) = call(sums_body, [((N_X * N_Z, 128), F32)], shared, res, name="sums")
    sums = swap(sums_msg, ROWS)
    near_x_msg, corr_2, sol, mine = call(
        second_body,
        [((N_X, RHS, BLOCK), BF16), (packed, F32), (packed, F32), (packed, F32)],
        sums,
        shared,
        res,
        corr,
        kern_b,
        noise,
        name="second",
    )
    near_x = swap(near_x_msg, X)
    (line_msg,) = call(apply_body, [((N_Z, *packed), F32)], near_x, kern, name="apply")
    flat = swap(line_msg, Z)
    near_msg, applied = call(
        last_sums_body,
        [((N_C, 128), F32), (packed, F32)],
        flat,
        corr_2,
        noise,
        mine,
        name="last_sums",
    )
    near = swap(near_msg, COLS)
    (sums_msg,) = call(gather_body, [((N_X * N_Z, 128), F32)], near, name="near")
    sums = swap(sums_msg, ROWS)
    return tuple(
        call(
            end_body,
            [((RHS, OWN), F32)] * 2,
            sums,
            applied,
            corr_2,
            sol,
            mine,
            name="end",
        )
    )


def solution(mesh):
    finer = Mesh(mesh.devices.reshape(N_X, N_Z, 4, 2), ROWS_COLS)
    in_specs = (P(None, ROWS_COLS), P(None, ROWS_COLS), P(ROWS_COLS), P(), P())
    out_specs = (P(None, ROWS_COLS), P(None, ROWS_COLS))
    return jax.shard_map(body, mesh=finer, in_specs=in_specs, out_specs=out_specs, check_vma=False)
```

```python
import jax
import jax.numpy as jnp
from jax import lax
from jax.experimental import pallas as pl
from jax.experimental.pallas import tpu as pltpu
from jax.sharding import Mesh
from jax.sharding import PartitionSpec as P

INNER = 3
X, Z, Y, K = "rows_0", "rows_1", "cols_0", "cols_1"
PLANE = (X, Y, K)
ROWS_COLS = (X, Z, Y, K)
N_X, N_Z, N_C = 4, 16, 8
FEATS, RHS, OWN, BLOCK = 16, 32, 64, 512
LINE, FLAT = N_Z * OWN, N_X * BLOCK
DEPTH = 7 * FEATS
ROOT_LOG2E = 1.4426950408889634**0.5
F32, BF16 = jnp.float32, jnp.bfloat16
PARAMS = pltpu.CompilerParams(vmem_limit_bytes=12 * 1024 * 1024)


def low_lanes(rows):
    return lax.broadcasted_iota(jnp.int32, (rows, 2 * OWN), 1) < OWN


def join(a, b):
    low = low_lanes(a.shape[0])
    top = jnp.where(low, a, pltpu.roll(b, OWN, 1))
    bottom = jnp.where(low, pltpu.roll(a, OWN, 1), b)
    return jnp.concatenate([top, bottom], axis=0)


def part(field):
    half = field.shape[0] // 2
    top, bottom = field[:half], field[half:]
    low = low_lanes(half)
    return (
        jnp.where(low, top, pltpu.roll(bottom, OWN, 1)),
        jnp.where(low, pltpu.roll(top, OWN, 1), bottom),
    )


def join_all(pieces):
    tiles = [join(a, b) for a, b in zip(pieces[0::2], pieces[1::2])]
    return jnp.concatenate(tiles, axis=1)


def part_all(field):
    pieces = []
    for at in range(0, field.shape[1], 2 * OWN):
        pieces += part(field[:, at : at + 2 * OWN])
    return pieces


def own_piece(pieces):
    me = lax.axis_index(PLANE)
    mine = jnp.zeros_like(pieces[0])
    for which, piece in enumerate(pieces):
        mine = jnp.where(me == which, piece, mine)
    return mine


def by_half(column):
    half = column.shape[0] // 2
    return jnp.where(low_lanes(half), column[:half], column[half:])


def three(value):
    first = value.astype(BF16).astype(F32)
    second = (value - first).astype(BF16).astype(F32)
    third = (value - first - second).astype(BF16).astype(F32)
    return first, second, third


def factors(parts, side):
    p1, p2, p3 = parts
    scaled = p1 + (p2 + p3)
    h1, h2, h3 = three(-0.5 * jnp.sum(scaled * scaled, axis=0, keepdims=True))
    row = lax.broadcasted_iota(jnp.int32, scaled.shape, 0)
    at = 0 if side == 0 else 3
    tail = jnp.where(row < 6, 1.0, 0.0)
    for offset, h in enumerate((h1, h2, h3)):
        tail = jnp.where(row == at + offset, h, tail)
    order = (p1, p1, p2, p2, p1, p3) if side == 0 else (p1, p2, p1, p2, p3, p1)
    return jnp.concatenate([*order, tail], axis=0).astype(BF16)


def block_cg(residual, kern, noise):
    remains, direction = residual, residual
    correction = jnp.zeros_like(residual)
    res_norm = jnp.sum(remains * remains, axis=1, keepdims=True)
    for turn in range(INNER):
        image = jnp.dot(direction.astype(BF16), kern, preferred_element_type=F32)
        image = image + noise * direction
        step = res_norm / jnp.sum(direction * image, axis=1, keepdims=True)
        correction = correction + step * direction
        remains = remains - step * image
        if turn + 1 < INNER:
            new_norm = jnp.sum(remains * remains, axis=1, keepdims=True)
            direction = remains + (new_norm / res_norm) * direction
            res_norm = new_norm
    return correction


def sums_row(residual, applied):
    lane = lax.broadcasted_iota(jnp.int32, (RHS, 128), 1)
    cross = jnp.sum(residual * applied, axis=1, keepdims=True)
    energy = jnp.sum(applied * applied, axis=1, keepdims=True)
    turned = jnp.where(lane == 0, cross, jnp.where(lane == 1, energy, 0.0)).T
    blank = jnp.zeros((1, 128 - 2 * RHS), F32)
    return jnp.concatenate([turned[0:1], turned[1:2], blank], axis=1)


def damping_of(rows):
    total = jnp.sum(rows, axis=0, keepdims=True)
    turned = jnp.broadcast_to(total, (8, 128)).T
    return turned[0:RHS, 0:1] / (turned[RHS : 2 * RHS, 0:1] + 1e-6)


def pack_body(
    feat_any, targ_any, order_any, scale_any, noise_any,
    plane_ref, line_ref, noise_ref,
    feat_ref, targ_ref, order_ref, scale_ref, given_ref, sems,
):
    pairs = (
        (scale_any, scale_ref),
        (noise_any, given_ref),
        (feat_any, feat_ref),
        (targ_any, targ_ref),
        (order_any, order_ref),
    )
    copies = [
        pltpu.make_async_copy(src, dst, sems.at[i]) for i, (src, dst) in enumerate(pairs)
    ]
    for copy in copies:
        copy.start()
    for copy in copies:
        copy.wait()

    def halves(field):
        half = field.shape[0] // 2
        return jnp.concatenate([field[:half], field[half:]], axis=1)

    def column(source, shape):
        row = lax.broadcasted_iota(jnp.int32, shape, 0)
        filled = jnp.zeros(shape, F32)
        for i in range(shape[0]):
            filled = jnp.where(row == i, source[i], filled)
        return filled

    scaled = halves(feat_ref[...] / column(scale_ref, (FEATS, OWN)) * ROOT_LOG2E)
    order = (order_ref[...] % BLOCK).astype(F32)
    order = jnp.concatenate([order, order], axis=1)
    order = jnp.broadcast_to(order, (8, 2 * OWN))
    whole = jnp.concatenate([scaled, halves(targ_ref[...]), order], axis=0)
    for to in range(N_X * N_C):
        plane_ref[to] = whole
    for to in range(N_Z):
        line_ref[to] = scaled
    noise_ref[...] = column(given_ref, (RHS, 128))


def cut(field, which):
    return field[:, which * BLOCK : (which + 1) * BLOCK]


def first_body(
    recv_ref, noise_ref, kern_ref, state_ref, mine_ref, own_ref, left_ref
):
    mine = []
    residuals = []
    for x in range(N_X):
        pieces = [recv_ref[x * N_C + i] for i in range(N_C)]
        parts = three(join_all([p[0:8] for p in pieces]))
        left = factors(parts, 0).T
        left_ref[pl.ds(x * BLOCK, BLOCK), :] = left
        exponent = jnp.dot(left, factors(parts, 1), preferred_element_type=F32)
        kern_ref[x] = jnp.exp2(exponent).astype(BF16)
        low = low_lanes(1)
        order = [
            jnp.where(low, a[24:25], b[24:25])
            for a, b in zip(pieces[0::2], pieces[1::2])
        ]
        order = jnp.concatenate(order, axis=1).astype(jnp.int32)
        index = lax.broadcasted_iota(jnp.int32, (BLOCK, BLOCK), 0)
        pick = jnp.where(index == order, 1.0, 0.0).astype(BF16)
        targets = three(join_all([p[8:24] for p in pieces]))
        stack = jnp.concatenate(targets, axis=0).astype(BF16)
        moved = jnp.dot(stack, pick, preferred_element_type=F32)
        residual = moved[0:RHS] + (moved[RHS : 2 * RHS] + moved[2 * RHS :])
        state_ref[0:RHS, pl.ds(x * BLOCK, BLOCK)] = residual
        correction = block_cg(residual, kern_ref[x], noise_ref[:, 0:1])
        state_ref[RHS:, pl.ds(x * BLOCK, BLOCK)] = correction
        mine += part_all(correction)
        residuals += part_all(residual)
    mine_ref[...] = own_piece(mine)
    own_ref[...] = own_piece(residuals)


def spread(msg_ref, at, field):
    for which, piece in enumerate(part_all(field)):
        msg_ref[at + which] = piece


TILE = min(LINE, 256)


def build_body(line_ref, left_ref, state_ref, msg_ref, kern_ref):
    packed = state_ref[RHS:, :].astype(BF16)
    for at in range(0, LINE, TILE):
        tiles = range(at // OWN, (at + TILE) // OWN, 2)
        field = jnp.concatenate([join(line_ref[i], line_ref[i + 1]) for i in tiles], axis=1)
        exponent = jnp.dot(
            left_ref[...], factors(three(field), 1), preferred_element_type=F32
        )
        kern = jnp.exp2(exponent).astype(BF16)
        kern_ref[:, pl.ds(at, TILE)] = kern
        moved = jnp.dot(packed, kern, preferred_element_type=F32)
        spread(msg_ref, at // OWN, moved)


def applied_of(recv_ref, corr_ref, noise_ref):
    total = recv_ref[0]
    for i in range(1, recv_ref.shape[0]):
        total = total + recv_ref[i]
    return total + by_half(noise_ref[:, 0:1]) * corr_ref[...]


def share_body(recv_ref, corr_ref, noise_ref, msg_ref):
    applied = applied_of(recv_ref, corr_ref, noise_ref)
    for to in range(N_X * N_C):
        msg_ref[to] = applied


def sums_body(recv_ref, res_ref, msg_ref, applied_ref):
    applied = join_all([recv_ref[i] for i in range(N_X * N_C)])
    applied_ref[...] = applied
    row = sums_row(res_ref[0:RHS, :], applied)
    msg_ref[...] = jnp.broadcast_to(row, msg_ref.shape)


def second_body(
    rows_ref, applied_ref, res_ref, block_ref, kern_ref, noise_ref, corr_ref, own_ref, near_ref,
    msg_ref, new_ref, sol_ref, mine_ref,
):
    damping = damping_of(rows_ref[...])
    residual = res_ref[0:RHS, :] - damping * applied_ref[...]
    corrections = [
        block_cg(cut(residual, x), block_ref[x], noise_ref[:, 0:1]) for x in range(N_X)
    ]
    correction = jnp.concatenate(corrections, axis=1)
    packed = correction.astype(BF16)
    for at in range(0, LINE, TILE):
        moved = jnp.dot(packed, kern_ref[:, pl.ds(at, TILE)], preferred_element_type=F32)
        spread(msg_ref, at // OWN, moved)
    new_ref[...] = own_piece(part_all(correction))
    sol_ref[...] = by_half(damping) * corr_ref[...]
    mine = own_piece([near_ref[i] for i in range(N_X * N_C)])
    mine_ref[...] = own_ref[...] - by_half(damping) * mine


def last_sums_body(recv_ref, corr_ref, noise_ref, mine_ref, msg_ref, applied_ref):
    applied = applied_of(recv_ref, corr_ref, noise_ref)
    applied_ref[...] = applied
    row = sums_row(split_halves(mine_ref[...]), split_halves(applied))
    msg_ref[...] = jnp.broadcast_to(row, msg_ref.shape)


def split_halves(field):
    return jnp.concatenate([field[:, :OWN], field[:, OWN:]], axis=0)


def gather_body(recv_ref, msg_ref):
    total = jnp.sum(recv_ref[...], axis=0, keepdims=True)
    msg_ref[...] = jnp.broadcast_to(total, msg_ref.shape)


def end_body(rows_ref, applied_ref, corr_ref, sol_ref, mine_ref, sol_out, res_out):
    damping = by_half(damping_of(rows_ref[...]))
    sol_out[...] = split_halves(sol_ref[...] + damping * corr_ref[...])
    res_out[...] = split_halves(mine_ref[...] - damping * applied_ref[...])


def call(body, outs, *args, scratch=(), space=pltpu.VMEM, flops=1 << 20, name):
    return pl.pallas_call(
        body,
        out_shape=[jax.ShapeDtypeStruct(s, d) for s, d in outs],
        in_specs=[pl.BlockSpec(memory_space=space)] * len(args),
        out_specs=[pl.BlockSpec(memory_space=pltpu.VMEM)] * len(outs),
        scratch_shapes=list(scratch),
        compiler_params=PARAMS,
        cost_estimate=pl.CostEstimate(flops=flops, transcendentals=0, bytes_accessed=1 << 20),
        name=name,
    )(*args)


def stay(array):
    return pltpu.with_memory_space_constraint(array, pltpu.HBM)


def swap(array, axis):
    return lax.all_to_all(array, axis, split_axis=0, concat_axis=0, tiled=True)


def body(features, targets, point_order, lengthscale, noise_var):
    packed = (RHS // 2, 2 * OWN)
    n_p = N_X * N_C
    plane_msg, feat_msg, noise = call(
        pack_body,
        [((n_p, 32, 128), F32), ((N_Z, 8, 128), F32), ((RHS, 128), F32)],
        *map(stay, (features, targets, point_order[None, :], lengthscale, noise_var)),
        scratch=[
            pltpu.VMEM((FEATS, OWN), F32),
            pltpu.VMEM((RHS, OWN), F32),
            pltpu.VMEM((1, OWN), jnp.int32),
            pltpu.SMEM((FEATS,), F32),
            pltpu.SMEM((RHS,), F32),
            pltpu.SemaphoreType.DMA((5,)),
        ],
        space=pltpu.HBM,
        name="pack",
    )
    plane = swap(plane_msg, PLANE)
    feat = swap(feat_msg, Z)
    blocks, state, corr, own, left = call(
        first_body,
        [
            ((N_X, BLOCK, BLOCK), BF16),
            ((2 * RHS, FLAT), F32),
            (packed, F32),
            (packed, F32),
            ((FLAT, DEPTH), BF16),
        ],
        plane,
        noise,
        flops=1 << 31,
        name="first",
    )
    line_msg, kern = call(
        build_body,
        [((N_Z, *packed), F32), ((FLAT, LINE), BF16)],
        feat,
        left,
        state,
        name="build",
    )
    line = swap(line_msg, Z)
    (share_msg,) = call(
        share_body, [((n_p, *packed), F32)], line, corr, noise, name="share"
    )
    shared = swap(share_msg, PLANE)
    sums_msg, applied = call(
        sums_body, [((N_Z, 128), F32), ((RHS, FLAT), F32)], shared, state, name="sums"
    )
    sums = swap(sums_msg, Z)
    line_msg, corr_2, sol, mine = call(
        second_body,
        [((N_Z, *packed), F32), (packed, F32), (packed, F32), (packed, F32)],
        sums,
        applied,
        state,
        blocks,
        kern,
        noise,
        corr,
        own,
        shared,
        name="second",
    )
    line = swap(line_msg, Z)
    near_msg, applied = call(
        last_sums_body,
        [((n_p, 128), F32), (packed, F32)],
        line,
        corr_2,
        noise,
        mine,
        name="last_sums",
    )
    near = swap(near_msg, PLANE)
    (sums_msg,) = call(gather_body, [((N_Z, 128), F32)], near, name="near")
    sums = swap(sums_msg, Z)
    return tuple(
        call(
            end_body,
            [((RHS, OWN), F32)] * 2,
            sums,
            applied,
            corr_2,
            sol,
            mine,
            name="end",
        )
    )


def solution(mesh):
    finer = Mesh(mesh.devices.reshape(N_X, N_Z, 4, 2), ROWS_COLS)
    in_specs = (P(None, ROWS_COLS), P(None, ROWS_COLS), P(ROWS_COLS), P(), P())
    out_specs = (P(None, ROWS_COLS), P(None, ROWS_COLS))
    return jax.shard_map(body, mesh=finer, in_specs=in_specs, out_specs=out_specs, check_vma=False)
```

```python
import jax
import jax.numpy as jnp
from jax import lax
from jax.experimental import pallas as pl
from jax.experimental.pallas import tpu as pltpu
from jax.sharding import Mesh
from jax.sharding import PartitionSpec as P

INNER = 3
X, Z, Y, K = "rows_0", "rows_1", "cols_0", "cols_1"
PLANE = (X, Y, K)
ROWS_COLS = (X, Z, Y, K)
N_X, N_Z, N_C = 4, 16, 8
FEATS, RHS, OWN, BLOCK = 16, 32, 64, 512
LINE, FLAT = N_Z * OWN, N_X * BLOCK
DEPTH = 7 * FEATS
ROOT_LOG2E = 1.4426950408889634**0.5
F32, BF16 = jnp.float32, jnp.bfloat16
PARAMS = pltpu.CompilerParams(vmem_limit_bytes=12 * 1024 * 1024)


def low_lanes(rows):
    return lax.broadcasted_iota(jnp.int32, (rows, 2 * OWN), 1) < OWN


def join(a, b):
    low = low_lanes(a.shape[0])
    top = jnp.where(low, a, pltpu.roll(b, OWN, 1))
    bottom = jnp.where(low, pltpu.roll(a, OWN, 1), b)
    return jnp.concatenate([top, bottom], axis=0)


def part(field):
    half = field.shape[0] // 2
    top, bottom = field[:half], field[half:]
    low = low_lanes(half)
    return (
        jnp.where(low, top, pltpu.roll(bottom, OWN, 1)),
        jnp.where(low, pltpu.roll(top, OWN, 1), bottom),
    )


def join_all(pieces):
    tiles = [join(a, b) for a, b in zip(pieces[0::2], pieces[1::2])]
    return jnp.concatenate(tiles, axis=1)


def part_all(field):
    pieces = []
    for at in range(0, field.shape[1], 2 * OWN):
        pieces += part(field[:, at : at + 2 * OWN])
    return pieces


def own_piece(pieces):
    me = lax.axis_index(PLANE)
    mine = jnp.zeros_like(pieces[0])
    for which, piece in enumerate(pieces):
        mine = jnp.where(me == which, piece, mine)
    return mine


def by_half(column):
    half = column.shape[0] // 2
    return jnp.where(low_lanes(half), column[:half], column[half:])


def three(value):
    first = value.astype(BF16).astype(F32)
    second = (value - first).astype(BF16).astype(F32)
    third = (value - first - second).astype(BF16).astype(F32)
    return first, second, third


def factors(parts, side):
    p1, p2, p3 = parts
    scaled = p1 + (p2 + p3)
    h1, h2, h3 = three(-0.5 * jnp.sum(scaled * scaled, axis=0, keepdims=True))
    row = lax.broadcasted_iota(jnp.int32, scaled.shape, 0)
    at = 0 if side == 0 else 3
    tail = jnp.where(row < 6, 1.0, 0.0)
    for offset, h in enumerate((h1, h2, h3)):
        tail = jnp.where(row == at + offset, h, tail)
    order = (p1, p1, p2, p2, p1, p3) if side == 0 else (p1, p2, p1, p2, p3, p1)
    return jnp.concatenate([*order, tail], axis=0).astype(BF16)


def plane_cg(residual, kern_ref, noise):
    def stack(field):
        return jnp.concatenate([cut(field, x) for x in range(N_X)], axis=0)

    def image_of(direction):
        packed = direction.astype(BF16)
        images = [
            jnp.dot(
                packed[x * RHS : (x + 1) * RHS], kern_ref[x], preferred_element_type=F32
            )
            for x in range(N_X)
        ]
        return jnp.concatenate(images, axis=0) + shift * direction

    shift = jnp.concatenate([noise] * N_X, axis=0)
    remains = direction = stack(residual)
    correction = jnp.zeros_like(remains)
    res_norm = jnp.sum(remains * remains, axis=1, keepdims=True)
    for turn in range(INNER):
        image = image_of(direction)
        step = res_norm / jnp.sum(direction * image, axis=1, keepdims=True)
        correction = correction + step * direction
        if turn + 1 < INNER:
            remains = remains - step * image
            new_norm = jnp.sum(remains * remains, axis=1, keepdims=True)
            direction = remains + (new_norm / res_norm) * direction
            res_norm = new_norm
    pieces = [correction[x * RHS : (x + 1) * RHS] for x in range(N_X)]
    return jnp.concatenate(pieces, axis=1)


def sums_row(residual, applied):
    lane = lax.broadcasted_iota(jnp.int32, (RHS, 128), 1)
    cross = jnp.sum(residual * applied, axis=1, keepdims=True)
    energy = jnp.sum(applied * applied, axis=1, keepdims=True)
    turned = jnp.where(lane == 0, cross, jnp.where(lane == 1, energy, 0.0)).T
    blank = jnp.zeros((1, 128 - 2 * RHS), F32)
    return jnp.concatenate([turned[0:1], turned[1:2], blank], axis=1)


def damping_of(rows):
    total = jnp.sum(rows, axis=0, keepdims=True)
    turned = jnp.broadcast_to(total, (8, 128)).T
    return turned[0:RHS, 0:1] / (turned[RHS : 2 * RHS, 0:1] + 1e-6)


def pack_body(
    feat_any, targ_any, order_any, scale_any, noise_any,
    plane_ref, line_ref, noise_ref,
    feat_ref, targ_ref, order_ref, scale_ref, given_ref, sems,
):
    pairs = (
        (scale_any, scale_ref),
        (noise_any, given_ref),
        (feat_any, feat_ref),
        (targ_any, targ_ref),
        (order_any, order_ref),
    )
    copies = [
        pltpu.make_async_copy(src, dst, sems.at[i]) for i, (src, dst) in enumerate(pairs)
    ]
    for copy in copies:
        copy.start()
    for copy in copies:
        copy.wait()

    def halves(field):
        half = field.shape[0] // 2
        return jnp.concatenate([field[:half], field[half:]], axis=1)

    def column(source, shape):
        row = lax.broadcasted_iota(jnp.int32, shape, 0)
        filled = jnp.zeros(shape, F32)
        for i in range(shape[0]):
            filled = jnp.where(row == i, source[i], filled)
        return filled

    scaled = halves(feat_ref[...] / column(scale_ref, (FEATS, OWN)) * ROOT_LOG2E)
    order = (order_ref[...] % BLOCK).astype(F32)
    order = jnp.concatenate([order, order], axis=1)
    order = jnp.broadcast_to(order, (8, 2 * OWN))
    whole = jnp.concatenate([scaled, halves(targ_ref[...]), order], axis=0)
    for to in range(N_X * N_C):
        plane_ref[to] = whole
    line_ref[...] = scaled
    noise_ref[...] = column(given_ref, (RHS, 128))


def cut(field, which):
    return field[:, which * BLOCK : (which + 1) * BLOCK]


def first_body(
    recv_ref, noise_ref, kern_ref, state_ref, mine_ref, own_ref, left_ref
):
    for x in range(N_X):
        pieces = [recv_ref[x * N_C + i] for i in range(N_C)]
        parts = three(join_all([p[0:8] for p in pieces]))
        left = factors(parts, 0).T
        left_ref[pl.ds(x * BLOCK, BLOCK), :] = left
        exponent = jnp.dot(left, factors(parts, 1), preferred_element_type=F32)
        kern_ref[x] = jnp.exp2(exponent).astype(BF16)
        low = low_lanes(1)
        order = [
            jnp.where(low, a[24:25], b[24:25])
            for a, b in zip(pieces[0::2], pieces[1::2])
        ]
        order = jnp.concatenate(order, axis=1).astype(jnp.int32)
        index = lax.broadcasted_iota(jnp.int32, (BLOCK, BLOCK), 0)
        pick = jnp.where(index == order, 1.0, 0.0).astype(BF16)
        targets = three(join_all([p[8:24] for p in pieces]))
        stack = jnp.concatenate(targets, axis=0).astype(BF16)
        moved = jnp.dot(stack, pick, preferred_element_type=F32)
        residual = moved[0:RHS] + (moved[RHS : 2 * RHS] + moved[2 * RHS :])
        state_ref[0:RHS, pl.ds(x * BLOCK, BLOCK)] = residual
    residual = state_ref[0:RHS, :]
    correction = plane_cg(residual, kern_ref, noise_ref[:, 0:1])
    state_ref[RHS:, :] = correction
    mine_ref[...] = own_piece(part_all(correction))
    own_ref[...] = own_piece(part_all(residual))


def spread(msg_ref, at, field):
    for which, piece in enumerate(part_all(field)):
        msg_ref[at + which] = piece


TILE = min(LINE, 256)


def build_body(line_ref, left_ref, state_ref, msg_ref, kern_ref):
    def piece(i):
        return line_ref[pl.ds(8 * i, 8), :]

    packed = state_ref[RHS:, :].astype(BF16)
    for at in range(0, LINE, TILE):
        tiles = range(at // OWN, (at + TILE) // OWN, 2)
        field = jnp.concatenate([join(piece(i), piece(i + 1)) for i in tiles], axis=1)
        exponent = jnp.dot(
            left_ref[...], factors(three(field), 1), preferred_element_type=F32
        )
        kern = jnp.exp2(exponent).astype(BF16)
        kern_ref[:, pl.ds(at, TILE)] = kern
        moved = jnp.dot(packed, kern, preferred_element_type=F32)
        spread(msg_ref, at // OWN, moved)


def applied_of(recv_ref, corr_ref, noise_ref):
    total = recv_ref[0]
    for i in range(1, recv_ref.shape[0]):
        total = total + recv_ref[i]
    return total + by_half(noise_ref[:, 0:1]) * corr_ref[...]


def share_body(recv_ref, corr_ref, noise_ref, msg_ref):
    applied = applied_of(recv_ref, corr_ref, noise_ref)
    for to in range(N_X * N_C):
        msg_ref[to] = applied


def sums_body(recv_ref, res_ref, msg_ref, applied_ref):
    applied = join_all([recv_ref[i] for i in range(N_X * N_C)])
    applied_ref[...] = applied
    row = sums_row(res_ref[0:RHS, :], applied)
    msg_ref[...] = jnp.broadcast_to(row, msg_ref.shape)


def second_body(
    rows_ref, applied_ref, res_ref, block_ref, kern_ref, noise_ref, corr_ref, own_ref, near_ref,
    msg_ref, new_ref, sol_ref, mine_ref,
):
    damping = damping_of(rows_ref[...])
    residual = res_ref[0:RHS, :] - damping * applied_ref[...]
    correction = plane_cg(residual, block_ref, noise_ref[:, 0:1])
    packed = correction.astype(BF16)
    for at in range(0, LINE, TILE):
        moved = jnp.dot(packed, kern_ref[:, pl.ds(at, TILE)], preferred_element_type=F32)
        spread(msg_ref, at // OWN, moved)
    new_ref[...] = own_piece(part_all(correction))
    sol_ref[...] = by_half(damping) * corr_ref[...]
    mine = own_piece([near_ref[i] for i in range(N_X * N_C)])
    mine_ref[...] = own_ref[...] - by_half(damping) * mine


def last_sums_body(recv_ref, corr_ref, noise_ref, mine_ref, msg_ref, applied_ref):
    applied = applied_of(recv_ref, corr_ref, noise_ref)
    applied_ref[...] = applied
    row = sums_row(split_halves(mine_ref[...]), split_halves(applied))
    msg_ref[...] = jnp.broadcast_to(row, msg_ref.shape)


def split_halves(field):
    return jnp.concatenate([field[:, :OWN], field[:, OWN:]], axis=0)


def gather_body(recv_ref, msg_ref):
    total = jnp.sum(recv_ref[...], axis=0, keepdims=True)
    msg_ref[...] = jnp.broadcast_to(total, msg_ref.shape)


def end_body(rows_ref, applied_ref, corr_ref, sol_ref, mine_ref, sol_out, res_out):
    damping = by_half(damping_of(rows_ref[...]))
    sol_out[...] = split_halves(sol_ref[...] + damping * corr_ref[...])
    res_out[...] = split_halves(mine_ref[...] - damping * applied_ref[...])


def call(body, outs, *args, scratch=(), space=pltpu.VMEM, flops=1 << 20, name):
    return pl.pallas_call(
        body,
        out_shape=[jax.ShapeDtypeStruct(s, d) for s, d in outs],
        in_specs=[pl.BlockSpec(memory_space=space)] * len(args),
        out_specs=[pl.BlockSpec(memory_space=pltpu.VMEM)] * len(outs),
        scratch_shapes=list(scratch),
        compiler_params=PARAMS,
        cost_estimate=pl.CostEstimate(flops=flops, transcendentals=0, bytes_accessed=1 << 20),
        name=name,
    )(*args)


def stay(array):
    return pltpu.with_memory_space_constraint(array, pltpu.HBM)


def swap(array, axis):
    return lax.all_to_all(array, axis, split_axis=0, concat_axis=0, tiled=True)


def body(features, targets, point_order, lengthscale, noise_var):
    packed = (RHS // 2, 2 * OWN)
    n_p = N_X * N_C
    plane_msg, feat_msg, noise = call(
        pack_body,
        [((n_p, 32, 128), F32), ((8, 128), F32), ((RHS, 128), F32)],
        *map(stay, (features, targets, point_order[None, :], lengthscale, noise_var)),
        scratch=[
            pltpu.VMEM((FEATS, OWN), F32),
            pltpu.VMEM((RHS, OWN), F32),
            pltpu.VMEM((1, OWN), jnp.int32),
            pltpu.SMEM((FEATS,), F32),
            pltpu.SMEM((RHS,), F32),
            pltpu.SemaphoreType.DMA((5,)),
        ],
        space=pltpu.HBM,
        name="pack",
    )
    plane = swap(plane_msg, PLANE)
    feat = lax.all_gather(feat_msg, Z, axis=0, tiled=True)
    blocks, state, corr, own, left = call(
        first_body,
        [
            ((N_X, BLOCK, BLOCK), BF16),
            ((2 * RHS, FLAT), F32),
            (packed, F32),
            (packed, F32),
            ((FLAT, DEPTH), BF16),
        ],
        plane,
        noise,
        flops=1 << 31,
        name="first",
    )
    line_msg, kern = call(
        build_body,
        [((N_Z, *packed), F32), ((FLAT, LINE), BF16)],
        feat,
        left,
        state,
        name="build",
    )
    line = swap(line_msg, Z)
    (share_msg,) = call(
        share_body, [((n_p, *packed), F32)], line, corr, noise, name="share"
    )
    shared = swap(share_msg, PLANE)
    sums_msg, applied = call(
        sums_body, [((N_Z, 128), F32), ((RHS, FLAT), F32)], shared, state, name="sums"
    )
    sums = swap(sums_msg, Z)
    line_msg, corr_2, sol, mine = call(
        second_body,
        [((N_Z, *packed), F32), (packed, F32), (packed, F32), (packed, F32)],
        sums,
        applied,
        state,
        blocks,
        kern,
        noise,
        corr,
        own,
        shared,
        name="second",
    )
    line = swap(line_msg, Z)
    near_msg, applied = call(
        last_sums_body,
        [((n_p, 128), F32), (packed, F32)],
        line,
        corr_2,
        noise,
        mine,
        name="last_sums",
    )
    near = swap(near_msg, PLANE)
    (sums_msg,) = call(gather_body, [((N_Z, 128), F32)], near, name="near")
    sums = swap(sums_msg, Z)
    return tuple(
        call(
            end_body,
            [((RHS, OWN), F32)] * 2,
            sums,
            applied,
            corr_2,
            sol,
            mine,
            name="end",
        )
    )


def solution(mesh):
    finer = Mesh(mesh.devices.reshape(N_X, N_Z, 4, 2), ROWS_COLS)
    in_specs = (P(None, ROWS_COLS), P(None, ROWS_COLS), P(ROWS_COLS), P(), P())
    out_specs = (P(None, ROWS_COLS), P(None, ROWS_COLS))
    return jax.shard_map(body, mesh=finer, in_specs=in_specs, out_specs=out_specs, check_vma=False)
```

```python
import jax
import jax.numpy as jnp
from jax import lax
from jax.experimental import pallas as pl
from jax.experimental.pallas import tpu as pltpu
from jax.sharding import Mesh
from jax.sharding import PartitionSpec as P

INNER = 3
X, Z, Y, K = "rows_0", "rows_1", "cols_0", "cols_1"
ROWS, COLS, PLANE = (X, Z), (Y, K), (X, Y, K)
ROWS_COLS = (X, Z, Y, K)
N_X, N_Z, N_C = 4, 16, 8
FEATS, RHS, OWN, BLOCK = 16, 32, 64, 512
LINE, FLAT = N_Z * OWN, N_X * BLOCK
DEPTH = 7 * FEATS
SENT = FEATS // 2 + RHS // 2 + 1
ROOT_LOG2E = 1.4426950408889634**0.5
F32, BF16 = jnp.float32, jnp.bfloat16
PARAMS = pltpu.CompilerParams(vmem_limit_bytes=12 * 1024 * 1024)


def low_lanes(rows):
    return lax.broadcasted_iota(jnp.int32, (rows, 2 * OWN), 1) < OWN


def join(a, b):
    low = low_lanes(a.shape[0])
    top = jnp.where(low, a, pltpu.roll(b, OWN, 1))
    bottom = jnp.where(low, pltpu.roll(a, OWN, 1), b)
    return jnp.concatenate([top, bottom], axis=0)


def part(field):
    half = field.shape[0] // 2
    top, bottom = field[:half], field[half:]
    low = low_lanes(half)
    return (
        jnp.where(low, top, pltpu.roll(bottom, OWN, 1)),
        jnp.where(low, pltpu.roll(top, OWN, 1), bottom),
    )


def join_all(pieces):
    tiles = [join(a, b) for a, b in zip(pieces[0::2], pieces[1::2])]
    return jnp.concatenate(tiles, axis=1)


def part_all(field):
    pieces = []
    for at in range(0, field.shape[1], 2 * OWN):
        pieces += part(field[:, at : at + 2 * OWN])
    return pieces


def own_piece(pieces):
    me = lax.axis_index(PLANE)
    mine = jnp.zeros_like(pieces[0])
    for which, piece in enumerate(pieces):
        mine = jnp.where(me == which, piece, mine)
    return mine


def by_half(column):
    half = column.shape[0] // 2
    return jnp.where(low_lanes(half), column[:half], column[half:])


def three(value):
    first = value.astype(BF16).astype(F32)
    second = (value - first).astype(BF16).astype(F32)
    third = (value - first - second).astype(BF16).astype(F32)
    return first, second, third


def factors(parts, side):
    p1, p2, p3 = parts
    scaled = p1 + (p2 + p3)
    h1, h2, h3 = three(-0.5 * jnp.sum(scaled * scaled, axis=0, keepdims=True))
    row = lax.broadcasted_iota(jnp.int32, scaled.shape, 0)
    at = 0 if side == 0 else 3
    tail = jnp.where(row < 6, 1.0, 0.0)
    for offset, h in enumerate((h1, h2, h3)):
        tail = jnp.where(row == at + offset, h, tail)
    order = (p1, p1, p2, p2, p1, p3) if side == 0 else (p1, p2, p1, p2, p3, p1)
    return jnp.concatenate([*order, tail], axis=0).astype(BF16)


def plane_cg(residual, kern_ref, noise):
    def stack(field):
        return jnp.concatenate([cut(field, x) for x in range(N_X)], axis=0)

    def image_of(direction):
        packed = direction.astype(BF16)
        images = [
            jnp.dot(
                packed[x * RHS : (x + 1) * RHS], kern_ref[x], preferred_element_type=F32
            )
            for x in range(N_X)
        ]
        return jnp.concatenate(images, axis=0) + shift * direction

    shift = jnp.concatenate([noise] * N_X, axis=0)
    remains = direction = stack(residual)
    correction = jnp.zeros_like(remains)
    res_norm = jnp.sum(remains * remains, axis=1, keepdims=True)
    for turn in range(INNER):
        image = image_of(direction)
        step = res_norm / jnp.sum(direction * image, axis=1, keepdims=True)
        correction = correction + step * direction
        if turn + 1 < INNER:
            remains = remains - step * image
            new_norm = jnp.sum(remains * remains, axis=1, keepdims=True)
            direction = remains + (new_norm / res_norm) * direction
            res_norm = new_norm
    pieces = [correction[x * RHS : (x + 1) * RHS] for x in range(N_X)]
    return jnp.concatenate(pieces, axis=1)


def sums_row(residual, applied):
    lane = lax.broadcasted_iota(jnp.int32, (RHS, 128), 1)
    cross = jnp.sum(residual * applied, axis=1, keepdims=True)
    energy = jnp.sum(applied * applied, axis=1, keepdims=True)
    turned = jnp.where(lane == 0, cross, jnp.where(lane == 1, energy, 0.0)).T
    blank = jnp.zeros((1, 128 - 2 * RHS), F32)
    return jnp.concatenate([turned[0:1], turned[1:2], blank], axis=1)


def damping_of(rows):
    total = jnp.sum(rows, axis=0, keepdims=True)
    turned = jnp.broadcast_to(total, (8, 128)).T
    return turned[0:RHS, 0:1] / (turned[RHS : 2 * RHS, 0:1] + 1e-6)


def column(source, shape):
    row = lax.broadcasted_iota(jnp.int32, shape, 0)
    filled = jnp.zeros(shape, F32)
    for i in range(shape[0]):
        filled = jnp.where(row == i, source[i], filled)
    return filled


SIDE = pl.ds(FLAT, 128)


def noise_of(state_ref):
    return state_ref[0:RHS, FLAT : FLAT + 1]


def own_correction(state_ref):
    return state_ref[RHS : RHS + RHS // 2, SIDE]


def own_residual(state_ref):
    return state_ref[RHS + RHS // 2 :, SIDE]


def pack_body(
    feat_any, targ_any, order_any, scale_any,
    plane_ref, line_ref,
    feat_ref, targ_ref, order_ref, scale_ref, sems,
):
    pairs = (
        (scale_any, scale_ref),
        (feat_any, feat_ref),
        (targ_any, targ_ref),
        (order_any, order_ref),
    )
    copies = [
        pltpu.make_async_copy(src, dst, sems.at[i]) for i, (src, dst) in enumerate(pairs)
    ]
    for copy in copies:
        copy.start()
    for copy in copies:
        copy.wait()

    def halves(field):
        half = field.shape[0] // 2
        return jnp.concatenate([field[:half], field[half:]], axis=1)

    scaled = halves(feat_ref[...] / column(scale_ref, (FEATS, OWN)) * ROOT_LOG2E)
    order = (order_ref[...] % BLOCK).astype(F32)
    order = jnp.concatenate([order, order], axis=1)
    whole = jnp.concatenate([scaled, halves(targ_ref[...]), order], axis=0)
    for to in range(N_X * N_C):
        plane_ref[pl.ds(SENT * to, SENT), :] = whole
    for to in range(N_Z):
        line_ref[to] = scaled


def cut(field, which):
    return field[:, which * BLOCK : (which + 1) * BLOCK]


def first_body(recv_ref, noise_any, kern_ref, state_ref, left_ref, given_ref, sem):
    copy = pltpu.make_async_copy(noise_any, given_ref, sem)
    copy.start()
    for x in range(N_X):
        at = x * N_C * SENT
        pieces = [recv_ref[pl.ds(at + i * SENT, SENT), :] for i in range(N_C)]
        parts = three(join_all([p[0:8] for p in pieces]))
        left = factors(parts, 0).T
        left_ref[pl.ds(x * BLOCK, BLOCK), :] = left
        exponent = jnp.dot(left, factors(parts, 1), preferred_element_type=F32)
        kern_ref[x] = jnp.exp2(exponent).astype(BF16)
        low = low_lanes(1)
        order = [
            jnp.where(low, a[24:25], b[24:25])
            for a, b in zip(pieces[0::2], pieces[1::2])
        ]
        order = jnp.concatenate(order, axis=1).astype(jnp.int32)
        index = lax.broadcasted_iota(jnp.int32, (BLOCK, BLOCK), 0)
        pick = jnp.where(index == order, 1.0, 0.0).astype(BF16)
        targets = three(join_all([p[8:24] for p in pieces]))
        stack = jnp.concatenate(targets, axis=0).astype(BF16)
        moved = jnp.dot(stack, pick, preferred_element_type=F32)
        residual = moved[0:RHS] + (moved[RHS : 2 * RHS] + moved[2 * RHS :])
        state_ref[0:RHS, pl.ds(x * BLOCK, BLOCK)] = residual
    copy.wait()
    noise = column(given_ref, (RHS, 128))
    state_ref[0:RHS, SIDE] = noise
    residual = state_ref[0:RHS, 0:FLAT]
    correction = plane_cg(residual, kern_ref, noise[:, 0:1])
    state_ref[RHS:, 0:FLAT] = correction
    both = [own_piece(part_all(field)) for field in (correction, residual)]
    state_ref[RHS:, SIDE] = jnp.concatenate(both, axis=0)


def spread(msg_ref, at, field):
    for which, piece in enumerate(part_all(field)):
        msg_ref[at + which] = piece


TILE = min(LINE, 256)


def build_body(line_ref, left_ref, state_ref, msg_ref, kern_ref):
    def piece(i):
        return line_ref[i]

    packed = state_ref[RHS:, 0:FLAT].astype(BF16)
    for at in range(0, LINE, TILE):
        tiles = range(at // OWN, (at + TILE) // OWN, 2)
        field = jnp.concatenate([join(piece(i), piece(i + 1)) for i in tiles], axis=1)
        exponent = jnp.dot(
            left_ref[...], factors(three(field), 1), preferred_element_type=F32
        )
        kern = jnp.exp2(exponent).astype(BF16)
        kern_ref[:, pl.ds(at, TILE)] = kern
        moved = jnp.dot(packed, kern, preferred_element_type=F32)
        spread(msg_ref, at // OWN, moved)


def applied_of(recv_ref, correction, state_ref):
    total = recv_ref[0]
    for i in range(1, recv_ref.shape[0]):
        total = total + recv_ref[i]
    return total + by_half(noise_of(state_ref)) * correction


def share_body(recv_ref, state_ref, msg_ref):
    applied = applied_of(recv_ref, own_correction(state_ref), state_ref)
    for to in range(N_X * N_C):
        msg_ref[to] = applied


def sums_body(recv_ref, state_ref, msg_ref, applied_ref):
    applied = join_all([recv_ref[i] for i in range(N_X * N_C)])
    applied_ref[...] = applied
    row = sums_row(state_ref[0:RHS, 0:FLAT], applied)
    msg_ref[...] = jnp.broadcast_to(row, msg_ref.shape)


def second_body(
    rows_ref, applied_ref, state_ref, block_ref, kern_ref, near_ref,
    msg_ref, new_ref, sol_ref, mine_ref,
):
    damping = damping_of(rows_ref[...])
    residual = state_ref[0:RHS, 0:FLAT] - damping * applied_ref[...]
    correction = plane_cg(residual, block_ref, noise_of(state_ref))
    packed = correction.astype(BF16)
    for at in range(0, LINE, TILE):
        moved = jnp.dot(packed, kern_ref[:, pl.ds(at, TILE)], preferred_element_type=F32)
        spread(msg_ref, at // OWN, moved)
    new_ref[...] = own_piece(part_all(correction))
    sol_ref[...] = by_half(damping) * own_correction(state_ref)
    mine = own_piece([near_ref[i] for i in range(N_X * N_C)])
    mine_ref[...] = own_residual(state_ref) - by_half(damping) * mine


def last_sums_body(recv_ref, corr_ref, state_ref, mine_ref, msg_ref, applied_ref):
    applied = applied_of(recv_ref, corr_ref[...], state_ref)
    applied_ref[...] = applied
    row = sums_row(split_halves(mine_ref[...]), split_halves(applied))
    msg_ref[...] = jnp.broadcast_to(row, msg_ref.shape)


def split_halves(field):
    return jnp.concatenate([field[:, :OWN], field[:, OWN:]], axis=0)


def gather_body(recv_ref, msg_ref):
    total = jnp.sum(recv_ref[...], axis=0, keepdims=True)
    msg_ref[...] = jnp.broadcast_to(total, msg_ref.shape)


def end_body(rows_ref, applied_ref, corr_ref, sol_ref, mine_ref, sol_out, res_out):
    damping = by_half(damping_of(rows_ref[...]))
    sol_out[...] = split_halves(sol_ref[...] + damping * corr_ref[...])
    res_out[...] = split_halves(mine_ref[...] - damping * applied_ref[...])


def call(body, outs, *args, scratch=(), spaces=None, flops=1 << 20, name):
    return pl.pallas_call(
        body,
        out_shape=[jax.ShapeDtypeStruct(s, d) for s, d in outs],
        in_specs=[
            pl.BlockSpec(memory_space=s) for s in spaces or (pltpu.VMEM,) * len(args)
        ],
        out_specs=[pl.BlockSpec(memory_space=pltpu.VMEM)] * len(outs),
        scratch_shapes=list(scratch),
        compiler_params=PARAMS,
        cost_estimate=pl.CostEstimate(flops=flops, transcendentals=0, bytes_accessed=1 << 20),
        name=name,
    )(*args)


def stay(array):
    return pltpu.with_memory_space_constraint(array, pltpu.HBM)


def swap(array, axis):
    return lax.all_to_all(array, axis, split_axis=0, concat_axis=0, tiled=True)


def body(features, targets, point_order, lengthscale, noise_var):
    packed = (RHS // 2, 2 * OWN)
    n_p = N_X * N_C
    plane_msg, feat_msg = call(
        pack_body,
        [((n_p * SENT, 128), F32), ((N_Z, 8, 128), F32)],
        *map(stay, (features, targets, point_order[None, :], lengthscale)),
        scratch=[
            pltpu.VMEM((FEATS, OWN), F32),
            pltpu.VMEM((RHS, OWN), F32),
            pltpu.VMEM((1, OWN), jnp.int32),
            pltpu.SMEM((FEATS,), F32),
            pltpu.SemaphoreType.DMA((4,)),
        ],
        spaces=(pltpu.HBM,) * 4,
        name="pack",
    )
    plane = swap(plane_msg.reshape(n_p, 1, SENT * 128), PLANE).reshape(n_p * SENT, 128)
    feat = swap(feat_msg, Z)
    blocks, state, left = call(
        first_body,
        [
            ((N_X, BLOCK, BLOCK), BF16),
            ((2 * RHS, FLAT + 128), F32),
            ((FLAT, DEPTH), BF16),
        ],
        plane,
        stay(noise_var),
        scratch=[pltpu.SMEM((RHS,), F32), pltpu.SemaphoreType.DMA],
        spaces=(pltpu.VMEM, pltpu.HBM),
        flops=1 << 31,
        name="first",
    )
    line_msg, kern = call(
        build_body,
        [((N_Z, *packed), F32), ((FLAT, LINE), BF16)],
        feat,
        left,
        state,
        name="build",
    )
    line = swap(line_msg, Z)
    (share_msg,) = call(
        share_body, [((n_p, *packed), F32)], line, state, name="share"
    )
    shared = swap(share_msg, PLANE)
    sums_msg, applied = call(
        sums_body, [((N_Z, 128), F32), ((RHS, FLAT), F32)], shared, state, name="sums"
    )
    sums = swap(sums_msg, Z)
    line_msg, corr_2, sol, mine = call(
        second_body,
        [((N_Z, *packed), F32), (packed, F32), (packed, F32), (packed, F32)],
        sums,
        applied,
        state,
        blocks,
        kern,
        shared,
        name="second",
    )
    line = swap(line_msg, Z)
    near_msg, applied = call(
        last_sums_body,
        [((N_C, 128), F32), (packed, F32)],
        line,
        corr_2,
        state,
        mine,
        name="last_sums",
    )
    near = swap(near_msg, COLS)
    (sums_msg,) = call(gather_body, [((N_X * N_Z, 128), F32)], near, name="near")
    sums = swap(sums_msg, ROWS)
    return tuple(
        call(
            end_body,
            [((RHS, OWN), F32)] * 2,
            sums,
            applied,
            corr_2,
            sol,
            mine,
            name="end",
        )
    )


def solution(mesh):
    finer = Mesh(mesh.devices.reshape(N_X, N_Z, 4, 2), ROWS_COLS)
    in_specs = (P(None, ROWS_COLS), P(None, ROWS_COLS), P(ROWS_COLS), P(), P())
    out_specs = (P(None, ROWS_COLS), P(None, ROWS_COLS))
    return jax.shard_map(body, mesh=finer, in_specs=in_specs, out_specs=out_specs, check_vma=False)
```

```python
import jax
import jax.numpy as jnp
from jax import lax
from jax.experimental import pallas as pl
from jax.experimental.pallas import tpu as pltpu
from jax.sharding import Mesh
from jax.sharding import PartitionSpec as P

INNER = 3
X, Z, Y, K = "rows_0", "rows_1", "cols_0", "cols_1"
PLANE = (X, Y, K)
ROWS_COLS = (X, Z, Y, K)
N_X, N_Z, N_C = 4, 16, 8
FEATS, RHS, OWN, BLOCK = 16, 32, 64, 512
LINE, FLAT = N_Z * OWN, N_X * BLOCK
DEPTH = 7 * FEATS
SENT = FEATS // 2 + RHS // 2 + 1
TILE = min(LINE, 256)
ROOT_LOG2E = 1.4426950408889634**0.5
F32, BF16 = jnp.float32, jnp.bfloat16
PARAMS = pltpu.CompilerParams(vmem_limit_bytes=12 * 1024 * 1024)


def low_lanes(rows):
    return lax.broadcasted_iota(jnp.int32, (rows, 2 * OWN), 1) < OWN


def join(a, b):
    low = low_lanes(a.shape[0])
    top = jnp.where(low, a, pltpu.roll(b, OWN, 1))
    bottom = jnp.where(low, pltpu.roll(a, OWN, 1), b)
    return jnp.concatenate([top, bottom], axis=0)


def part(field):
    half = field.shape[0] // 2
    top, bottom = field[:half], field[half:]
    low = low_lanes(half)
    return (
        jnp.where(low, top, pltpu.roll(bottom, OWN, 1)),
        jnp.where(low, pltpu.roll(top, OWN, 1), bottom),
    )


def join_all(pieces):
    tiles = [join(a, b) for a, b in zip(pieces[0::2], pieces[1::2])]
    return jnp.concatenate(tiles, axis=1)


def part_all(field):
    pieces = []
    for at in range(0, field.shape[1], 2 * OWN):
        pieces += part(field[:, at : at + 2 * OWN])
    return pieces


def own_piece(pieces):
    me = lax.axis_index(PLANE)
    mine = jnp.zeros_like(pieces[0])
    for which, piece in enumerate(pieces):
        mine = jnp.where(me == which, piece, mine)
    return mine


def by_half(column):
    half = column.shape[0] // 2
    return jnp.where(low_lanes(half), column[:half], column[half:])


def three(value):
    first = value.astype(BF16).astype(F32)
    second = (value - first).astype(BF16).astype(F32)
    third = (value - first - second).astype(BF16).astype(F32)
    return first, second, third


def factors(parts, side):
    p1, p2, p3 = parts
    scaled = p1 + (p2 + p3)
    h1, h2, h3 = three(-0.5 * jnp.sum(scaled * scaled, axis=0, keepdims=True))
    row = lax.broadcasted_iota(jnp.int32, scaled.shape, 0)
    at = 0 if side == 0 else 3
    tail = jnp.where(row < 6, 1.0, 0.0)
    for offset, h in enumerate((h1, h2, h3)):
        tail = jnp.where(row == at + offset, h, tail)
    order = (p1, p1, p2, p2, p1, p3) if side == 0 else (p1, p2, p1, p2, p3, p1)
    return jnp.concatenate([*order, tail], axis=0).astype(BF16)


def plane_cg(residual, kern_ref, noise, beside=None):
    def stack(field):
        return jnp.concatenate([cut(field, x) for x in range(N_X)], axis=0)

    def image_of(direction):
        packed = direction.astype(BF16)
        images = [
            jnp.dot(
                packed[x * RHS : (x + 1) * RHS], kern_ref[x], preferred_element_type=F32
            )
            for x in range(N_X)
        ]
        return jnp.concatenate(images, axis=0) + shift * direction

    shift = jnp.concatenate([noise] * N_X, axis=0)
    remains = direction = stack(residual)
    correction = jnp.zeros_like(remains)
    res_norm = jnp.sum(remains * remains, axis=1, keepdims=True)
    for turn in range(INNER):
        image = image_of(direction)
        if beside is not None:
            beside(turn)
        step = res_norm / jnp.sum(direction * image, axis=1, keepdims=True)
        correction = correction + step * direction
        if turn + 1 < INNER:
            remains = remains - step * image
            new_norm = jnp.sum(remains * remains, axis=1, keepdims=True)
            direction = remains + (new_norm / res_norm) * direction
            res_norm = new_norm
    pieces = [correction[x * RHS : (x + 1) * RHS] for x in range(N_X)]
    return jnp.concatenate(pieces, axis=1)


def sums_row(residual, applied):
    lane = lax.broadcasted_iota(jnp.int32, (RHS, 128), 1)
    cross = jnp.sum(residual * applied, axis=1, keepdims=True)
    energy = jnp.sum(applied * applied, axis=1, keepdims=True)
    turned = jnp.where(lane == 0, cross, jnp.where(lane == 1, energy, 0.0)).T
    blank = jnp.zeros((1, 128 - 2 * RHS), F32)
    return jnp.concatenate([turned[0:1], turned[1:2], blank], axis=1)


def damping_of(rows):
    total = jnp.sum(rows, axis=0, keepdims=True)
    turned = jnp.broadcast_to(total, (8, 128)).T
    return turned[0:RHS, 0:1] / (turned[RHS : 2 * RHS, 0:1] + 1e-6)


def column(source, shape):
    row = lax.broadcasted_iota(jnp.int32, shape, 0)
    filled = jnp.zeros(shape, F32)
    for i in range(shape[0]):
        filled = jnp.where(row == i, source[i], filled)
    return filled


SIDE = pl.ds(FLAT, 128)


def noise_of(state_ref):
    return state_ref[0:RHS, FLAT : FLAT + 1]


def own_correction(state_ref):
    return state_ref[RHS : RHS + RHS // 2, SIDE]


def own_residual(state_ref):
    return state_ref[RHS + RHS // 2 :, SIDE]


def pack_body(
    feat_any, targ_any, order_any, scale_any,
    plane_ref, line_ref,
    feat_ref, targ_ref, order_ref, scale_ref, sems,
):
    pairs = (
        (scale_any, scale_ref),
        (feat_any, feat_ref),
        (targ_any, targ_ref),
        (order_any, order_ref),
    )
    copies = [
        pltpu.make_async_copy(src, dst, sems.at[i]) for i, (src, dst) in enumerate(pairs)
    ]
    for copy in copies:
        copy.start()
    for copy in copies:
        copy.wait()

    def halves(field):
        half = field.shape[0] // 2
        return jnp.concatenate([field[:half], field[half:]], axis=1)

    scaled = halves(feat_ref[...] / column(scale_ref, (FEATS, OWN)) * ROOT_LOG2E)
    order = (order_ref[...] % BLOCK).astype(F32)
    order = jnp.concatenate([order, order], axis=1)
    whole = jnp.concatenate([scaled, halves(targ_ref[...]), order], axis=0)
    for to in range(N_X * N_C):
        plane_ref[pl.ds(SENT * to, SENT), :] = whole
    for to in range(N_Z):
        line_ref[to] = scaled


def cut(field, which):
    return field[:, which * BLOCK : (which + 1) * BLOCK]


def first_body(
    recv_ref, line_ref, noise_any, kern_ref, state_ref, tile_ref, msg_ref, left_ref, given_ref, sem
):
    copy = pltpu.make_async_copy(noise_any, given_ref, sem)
    copy.start()
    tiles = range(0, LINE, TILE)

    def build(turn):
        for at in tiles[turn :: INNER + 1]:
            around = range(at // OWN, (at + TILE) // OWN, 2)
            pairs = [join(line_ref[i], line_ref[i + 1]) for i in around]
            right = factors(three(jnp.concatenate(pairs, axis=1)), 1)
            exponent = jnp.dot(left_ref[...], right, preferred_element_type=F32)
            tile_ref[:, pl.ds(at, TILE)] = jnp.exp2(exponent).astype(BF16)

    for x in range(N_X):
        at = x * N_C * SENT
        pieces = [recv_ref[pl.ds(at + i * SENT, SENT), :] for i in range(N_C)]
        parts = three(join_all([p[0:8] for p in pieces]))
        left = factors(parts, 0).T
        left_ref[pl.ds(x * BLOCK, BLOCK), :] = left
        exponent = jnp.dot(left, factors(parts, 1), preferred_element_type=F32)
        kern_ref[x] = jnp.exp2(exponent).astype(BF16)
        low = low_lanes(1)
        order = [
            jnp.where(low, a[24:25], b[24:25])
            for a, b in zip(pieces[0::2], pieces[1::2])
        ]
        order = jnp.concatenate(order, axis=1).astype(jnp.int32)
        index = lax.broadcasted_iota(jnp.int32, (BLOCK, BLOCK), 0)
        pick = jnp.where(index == order, 1.0, 0.0).astype(BF16)
        targets = three(join_all([p[8:24] for p in pieces]))
        stack = jnp.concatenate(targets, axis=0).astype(BF16)
        moved = jnp.dot(stack, pick, preferred_element_type=F32)
        residual = moved[0:RHS] + (moved[RHS : 2 * RHS] + moved[2 * RHS :])
        state_ref[0:RHS, pl.ds(x * BLOCK, BLOCK)] = residual
    copy.wait()
    noise = column(given_ref, (RHS, 128))
    state_ref[0:RHS, SIDE] = noise
    residual = state_ref[0:RHS, 0:FLAT]
    build(INNER)
    correction = plane_cg(residual, kern_ref, noise[:, 0:1], build)
    state_ref[RHS:, 0:FLAT] = correction
    both = [own_piece(part_all(field)) for field in (correction, residual)]
    state_ref[RHS:, SIDE] = jnp.concatenate(both, axis=0)
    apply(correction.astype(BF16), tile_ref, msg_ref)


def spread(msg_ref, at, field):
    for which, piece in enumerate(part_all(field)):
        msg_ref[at + which] = piece


def apply(packed, tile_ref, msg_ref):
    for at in range(0, LINE, TILE):
        moved = jnp.dot(packed, tile_ref[:, pl.ds(at, TILE)], preferred_element_type=F32)
        spread(msg_ref, at // OWN, moved)


def applied_of(recv_ref, correction, state_ref):
    total = recv_ref[0]
    for i in range(1, recv_ref.shape[0]):
        total = total + recv_ref[i]
    return total + by_half(noise_of(state_ref)) * correction


def share_body(recv_ref, state_ref, msg_ref):
    applied = applied_of(recv_ref, own_correction(state_ref), state_ref)
    for to in range(N_X * N_C):
        msg_ref[to] = applied


def sums_body(recv_ref, state_ref, msg_ref, applied_ref):
    applied = join_all([recv_ref[i] for i in range(N_X * N_C)])
    applied_ref[...] = applied
    row = sums_row(state_ref[0:RHS, 0:FLAT], applied)
    msg_ref[...] = jnp.broadcast_to(row, msg_ref.shape)


def second_body(
    rows_ref, applied_ref, state_ref, block_ref, kern_ref, near_ref,
    msg_ref, new_ref, sol_ref, mine_ref,
):
    damping = damping_of(rows_ref[...])
    residual = state_ref[0:RHS, 0:FLAT] - damping * applied_ref[...]
    correction = plane_cg(residual, block_ref, noise_of(state_ref))
    apply(correction.astype(BF16), kern_ref, msg_ref)
    new_ref[...] = own_piece(part_all(correction))
    sol_ref[...] = by_half(damping) * own_correction(state_ref)
    mine = own_piece([near_ref[i] for i in range(N_X * N_C)])
    mine_ref[...] = own_residual(state_ref) - by_half(damping) * mine


def last_sums_body(recv_ref, corr_ref, state_ref, mine_ref, msg_ref, applied_ref):
    applied = applied_of(recv_ref, corr_ref[...], state_ref)
    applied_ref[...] = applied
    row = sums_row(split_halves(mine_ref[...]), split_halves(applied))
    msg_ref[...] = jnp.broadcast_to(row, msg_ref.shape)


def split_halves(field):
    return jnp.concatenate([field[:, :OWN], field[:, OWN:]], axis=0)


def gather_body(recv_ref, msg_ref):
    total = jnp.sum(recv_ref[...], axis=0, keepdims=True)
    msg_ref[...] = jnp.broadcast_to(total, msg_ref.shape)


def end_body(rows_ref, applied_ref, corr_ref, sol_ref, mine_ref, sol_out, res_out):
    damping = by_half(damping_of(rows_ref[...]))
    sol_out[...] = split_halves(sol_ref[...] + damping * corr_ref[...])
    res_out[...] = split_halves(mine_ref[...] - damping * applied_ref[...])


def call(body, outs, *args, scratch=(), spaces=None, flops=1 << 20, name):
    return pl.pallas_call(
        body,
        out_shape=[jax.ShapeDtypeStruct(s, d) for s, d in outs],
        in_specs=[
            pl.BlockSpec(memory_space=s) for s in spaces or (pltpu.VMEM,) * len(args)
        ],
        out_specs=[pl.BlockSpec(memory_space=pltpu.VMEM)] * len(outs),
        scratch_shapes=list(scratch),
        compiler_params=PARAMS,
        cost_estimate=pl.CostEstimate(flops=flops, transcendentals=0, bytes_accessed=1 << 20),
        name=name,
    )(*args)


def stay(array):
    return pltpu.with_memory_space_constraint(array, pltpu.HBM)


def swap(array, axis):
    return lax.all_to_all(array, axis, split_axis=0, concat_axis=0, tiled=True)


def body(features, targets, point_order, lengthscale, noise_var):
    packed = (RHS // 2, 2 * OWN)
    n_p = N_X * N_C
    plane_msg, feat_msg = call(
        pack_body,
        [((n_p * SENT, 128), F32), ((N_Z, 8, 128), F32)],
        *map(stay, (features, targets, point_order[None, :], lengthscale)),
        scratch=[
            pltpu.VMEM((FEATS, OWN), F32),
            pltpu.VMEM((RHS, OWN), F32),
            pltpu.VMEM((1, OWN), jnp.int32),
            pltpu.SMEM((FEATS,), F32),
            pltpu.SemaphoreType.DMA((4,)),
        ],
        spaces=(pltpu.HBM,) * 4,
        name="pack",
    )
    plane = swap(plane_msg.reshape(n_p, 1, SENT * 128), PLANE).reshape(n_p * SENT, 128)
    feat = swap(feat_msg, Z)
    blocks, state, kern, line_msg = call(
        first_body,
        [
            ((N_X, BLOCK, BLOCK), BF16),
            ((2 * RHS, FLAT + 128), F32),
            ((FLAT, LINE), BF16),
            ((N_Z, *packed), F32),
        ],
        plane,
        feat,
        stay(noise_var),
        scratch=[
            pltpu.VMEM((FLAT, DEPTH), BF16),
            pltpu.SMEM((RHS,), F32),
            pltpu.SemaphoreType.DMA,
        ],
        spaces=(pltpu.VMEM, pltpu.VMEM, pltpu.HBM),
        name="first",
    )
    line = swap(line_msg, Z)
    (share_msg,) = call(
        share_body, [((n_p, *packed), F32)], line, state, name="share"
    )
    shared = swap(share_msg, PLANE)
    sums_msg, applied = call(
        sums_body, [((N_Z, 128), F32), ((RHS, FLAT), F32)], shared, state, name="sums"
    )
    sums = swap(sums_msg, Z)
    line_msg, corr_2, sol, mine = call(
        second_body,
        [((N_Z, *packed), F32), (packed, F32), (packed, F32), (packed, F32)],
        sums,
        applied,
        state,
        blocks,
        kern,
        shared,
        name="second",
    )
    line = swap(line_msg, Z)
    near_msg, applied = call(
        last_sums_body,
        [((n_p, 128), F32), (packed, F32)],
        line,
        corr_2,
        state,
        mine,
        name="last_sums",
    )
    near = swap(near_msg, PLANE)
    (sums_msg,) = call(gather_body, [((N_Z, 128), F32)], near, name="near")
    sums = swap(sums_msg, Z)
    return tuple(
        call(
            end_body,
            [((RHS, OWN), F32)] * 2,
            sums,
            applied,
            corr_2,
            sol,
            mine,
            name="end",
        )
    )


def solution(mesh):
    finer = Mesh(mesh.devices.reshape(N_X, N_Z, 4, 2), ROWS_COLS)
    in_specs = (P(None, ROWS_COLS), P(None, ROWS_COLS), P(ROWS_COLS), P(), P())
    out_specs = (P(None, ROWS_COLS), P(None, ROWS_COLS))
    return jax.shard_map(body, mesh=finer, in_specs=in_specs, out_specs=out_specs, check_vma=False)
```

```python
import jax
import jax.numpy as jnp
from jax import lax
from jax.experimental import pallas as pl
from jax.experimental.pallas import tpu as pltpu
from jax.sharding import Mesh
from jax.sharding import PartitionSpec as P

INNER = 3
X, Z, Y, K = "rows_0", "rows_1", "cols_0", "cols_1"
PLANE = (X, Y, K)
ROWS_COLS = (X, Z, Y, K)
N_X, N_Z, N_C = 4, 16, 8
FEATS, RHS, OWN, BLOCK = 16, 32, 64, 512
LINE, FLAT = N_Z * OWN, N_X * BLOCK
DEPTH = 7 * FEATS
SENT = FEATS // 2 + RHS // 2 + 1
ROOT_LOG2E = 1.4426950408889634**0.5
F32, BF16 = jnp.float32, jnp.bfloat16
PARAMS = pltpu.CompilerParams(vmem_limit_bytes=12 * 1024 * 1024)


def low_lanes(rows):
    return lax.broadcasted_iota(jnp.int32, (rows, 2 * OWN), 1) < OWN


def join(a, b):
    low = low_lanes(a.shape[0])
    top = jnp.where(low, a, pltpu.roll(b, OWN, 1))
    bottom = jnp.where(low, pltpu.roll(a, OWN, 1), b)
    return jnp.concatenate([top, bottom], axis=0)


def part(field):
    half = field.shape[0] // 2
    top, bottom = field[:half], field[half:]
    low = low_lanes(half)
    return (
        jnp.where(low, top, pltpu.roll(bottom, OWN, 1)),
        jnp.where(low, pltpu.roll(top, OWN, 1), bottom),
    )


def join_all(pieces):
    tiles = [join(a, b) for a, b in zip(pieces[0::2], pieces[1::2])]
    return jnp.concatenate(tiles, axis=1)


def part_all(field):
    pieces = []
    for at in range(0, field.shape[1], 2 * OWN):
        pieces += part(field[:, at : at + 2 * OWN])
    return pieces


def own_piece(pieces):
    me = lax.axis_index(PLANE)
    mine = jnp.zeros_like(pieces[0])
    for which, piece in enumerate(pieces):
        mine = jnp.where(me == which, piece, mine)
    return mine


def by_half(column):
    half = column.shape[0] // 2
    return jnp.where(low_lanes(half), column[:half], column[half:])


def three(value):
    first = value.astype(BF16).astype(F32)
    second = (value - first).astype(BF16).astype(F32)
    third = (value - first - second).astype(BF16).astype(F32)
    return first, second, third


def factors(parts, side):
    p1, p2, p3 = parts
    scaled = p1 + (p2 + p3)
    h1, h2, h3 = three(-0.5 * jnp.sum(scaled * scaled, axis=0, keepdims=True))
    row = lax.broadcasted_iota(jnp.int32, scaled.shape, 0)
    at = 0 if side == 0 else 3
    tail = jnp.where(row < 6, 1.0, 0.0)
    for offset, h in enumerate((h1, h2, h3)):
        tail = jnp.where(row == at + offset, h, tail)
    order = (p1, p1, p2, p2, p1, p3) if side == 0 else (p1, p2, p1, p2, p3, p1)
    return jnp.concatenate([*order, tail], axis=0).astype(BF16)


def plane_cg(residual, kern_ref, noise):
    def stack(field):
        return jnp.concatenate([cut(field, x) for x in range(N_X)], axis=0)

    def image_of(direction):
        packed = direction.astype(BF16)
        images = [
            jnp.dot(
                packed[x * RHS : (x + 1) * RHS], kern_ref[x], preferred_element_type=F32
            )
            for x in range(N_X)
        ]
        return jnp.concatenate(images, axis=0) + shift * direction

    shift = jnp.concatenate([noise] * N_X, axis=0)
    remains = direction = stack(residual)
    correction = jnp.zeros_like(remains)
    res_norm = jnp.sum(remains * remains, axis=1, keepdims=True)
    for turn in range(INNER):
        image = image_of(direction)
        step = res_norm / jnp.sum(direction * image, axis=1, keepdims=True)
        correction = correction + step * direction
        if turn + 1 < INNER:
            remains = remains - step * image
            new_norm = jnp.sum(remains * remains, axis=1, keepdims=True)
            direction = remains + (new_norm / res_norm) * direction
            res_norm = new_norm
    pieces = [correction[x * RHS : (x + 1) * RHS] for x in range(N_X)]
    return jnp.concatenate(pieces, axis=1)


def sums_row(residual, applied):
    lane = lax.broadcasted_iota(jnp.int32, (RHS, 128), 1)
    cross = jnp.sum(residual * applied, axis=1, keepdims=True)
    energy = jnp.sum(applied * applied, axis=1, keepdims=True)
    turned = jnp.where(lane == 0, cross, jnp.where(lane == 1, energy, 0.0)).T
    blank = jnp.zeros((1, 128 - 2 * RHS), F32)
    return jnp.concatenate([turned[0:1], turned[1:2], blank], axis=1)


def damping_of(rows):
    total = jnp.sum(rows, axis=0, keepdims=True)
    turned = jnp.broadcast_to(total, (8, 128)).T
    return turned[0:RHS, 0:1] / (turned[RHS : 2 * RHS, 0:1] + 1e-6)


def column(source, shape):
    row = lax.broadcasted_iota(jnp.int32, shape, 0)
    filled = jnp.zeros(shape, F32)
    for i in range(shape[0]):
        filled = jnp.where(row == i, source[i], filled)
    return filled


SIDE = pl.ds(FLAT, 128)


def noise_of(state_ref):
    return state_ref[0:RHS, FLAT : FLAT + 1]


def own_correction(state_ref):
    return state_ref[RHS : RHS + RHS // 2, SIDE]


def own_residual(state_ref):
    return state_ref[RHS + RHS // 2 :, SIDE]


def pack_body(
    feat_any, targ_any, order_any, scale_any,
    plane_ref, line_ref,
    feat_ref, targ_ref, order_ref, scale_ref, sems,
):
    pairs = (
        (scale_any, scale_ref),
        (feat_any, feat_ref),
        (targ_any, targ_ref),
        (order_any, order_ref),
    )
    copies = [
        pltpu.make_async_copy(src, dst, sems.at[i]) for i, (src, dst) in enumerate(pairs)
    ]
    for copy in copies:
        copy.start()
    for copy in copies:
        copy.wait()

    def halves(field):
        half = field.shape[0] // 2
        return jnp.concatenate([field[:half], field[half:]], axis=1)

    scaled = halves(feat_ref[...] / column(scale_ref, (FEATS, OWN)) * ROOT_LOG2E)
    order = (order_ref[...] % BLOCK).astype(F32)
    order = jnp.concatenate([order, order], axis=1)
    whole = jnp.concatenate([scaled, halves(targ_ref[...]), order], axis=0)
    for to in range(N_X * N_C):
        plane_ref[pl.ds(SENT * to, SENT), :] = whole
    for to in range(N_Z):
        line_ref[to] = scaled


def cut(field, which):
    return field[:, which * BLOCK : (which + 1) * BLOCK]


def first_body(recv_ref, noise_any, kern_ref, state_ref, left_ref, given_ref, sem):
    copy = pltpu.make_async_copy(noise_any, given_ref, sem)
    copy.start()
    for x in range(N_X):
        at = x * N_C * SENT
        pieces = [recv_ref[pl.ds(at + i * SENT, SENT), :] for i in range(N_C)]
        parts = three(join_all([p[0:8] for p in pieces]))
        left = factors(parts, 0).T
        left_ref[pl.ds(x * BLOCK, BLOCK), :] = left
        exponent = jnp.dot(left, factors(parts, 1), preferred_element_type=F32)
        kern_ref[x] = jnp.exp2(exponent).astype(BF16)
        low = low_lanes(1)
        order = [
            jnp.where(low, a[24:25], b[24:25])
            for a, b in zip(pieces[0::2], pieces[1::2])
        ]
        order = jnp.concatenate(order, axis=1).astype(jnp.int32)
        index = lax.broadcasted_iota(jnp.int32, (BLOCK, BLOCK), 0)
        pick = jnp.where(index == order, 1.0, 0.0).astype(BF16)
        targets = three(join_all([p[8:24] for p in pieces]))
        stack = jnp.concatenate(targets, axis=0).astype(BF16)
        moved = jnp.dot(stack, pick, preferred_element_type=F32)
        residual = moved[0:RHS] + (moved[RHS : 2 * RHS] + moved[2 * RHS :])
        state_ref[0:RHS, pl.ds(x * BLOCK, BLOCK)] = residual
    copy.wait()
    noise = column(given_ref, (RHS, 128))
    state_ref[0:RHS, SIDE] = noise
    residual = state_ref[0:RHS, 0:FLAT]
    correction = plane_cg(residual, kern_ref, noise[:, 0:1])
    state_ref[RHS:, 0:FLAT] = correction
    both = [own_piece(part_all(field)) for field in (correction, residual)]
    state_ref[RHS:, SIDE] = jnp.concatenate(both, axis=0)


def spread(msg_ref, at, field):
    for which, piece in enumerate(part_all(field)):
        msg_ref[at + which] = piece


TILE = min(LINE, 256)


def build_body(line_ref, left_ref, state_ref, msg_ref, kern_ref):
    def piece(i):
        return line_ref[i]

    packed = state_ref[RHS:, 0:FLAT].astype(BF16)
    for at in range(0, LINE, TILE):
        tiles = range(at // OWN, (at + TILE) // OWN, 2)
        field = jnp.concatenate([join(piece(i), piece(i + 1)) for i in tiles], axis=1)
        exponent = jnp.dot(
            left_ref[...], factors(three(field), 1), preferred_element_type=F32
        )
        kern = jnp.exp2(exponent).astype(BF16)
        kern_ref[:, pl.ds(at, TILE)] = kern
        moved = jnp.dot(packed, kern, preferred_element_type=F32)
        spread(msg_ref, at // OWN, moved)


def applied_of(recv_ref, correction, state_ref):
    total = recv_ref[0]
    for i in range(1, recv_ref.shape[0]):
        total = total + recv_ref[i]
    return total + by_half(noise_of(state_ref)) * correction


def share_body(recv_ref, state_ref, msg_ref):
    applied = applied_of(recv_ref, own_correction(state_ref), state_ref)
    for to in range(N_X * N_C):
        msg_ref[to] = applied


def sums_body(recv_ref, state_ref, msg_ref, applied_ref):
    applied = join_all([recv_ref[i] for i in range(N_X * N_C)])
    applied_ref[...] = applied
    row = sums_row(state_ref[0:RHS, 0:FLAT], applied)
    msg_ref[...] = jnp.broadcast_to(row, msg_ref.shape)


def second_body(
    rows_ref, applied_ref, state_ref, block_ref, kern_ref, near_ref,
    msg_ref, new_ref, sol_ref, mine_ref,
):
    damping = damping_of(rows_ref[...])
    residual = state_ref[0:RHS, 0:FLAT] - damping * applied_ref[...]
    correction = plane_cg(residual, block_ref, noise_of(state_ref))
    packed = correction.astype(BF16)
    for at in range(0, LINE, TILE):
        moved = jnp.dot(packed, kern_ref[:, pl.ds(at, TILE)], preferred_element_type=F32)
        spread(msg_ref, at // OWN, moved)
    new_ref[...] = own_piece(part_all(correction))
    sol_ref[...] = by_half(damping) * own_correction(state_ref)
    mine = own_piece([near_ref[i] for i in range(N_X * N_C)])
    mine_ref[...] = own_residual(state_ref) - by_half(damping) * mine


def last_sums_body(recv_ref, corr_ref, state_ref, mine_ref, msg_ref, applied_ref):
    applied = applied_of(recv_ref, corr_ref[...], state_ref)
    applied_ref[...] = applied
    row = sums_row(split_halves(mine_ref[...]), split_halves(applied))
    msg_ref[...] = jnp.broadcast_to(row, msg_ref.shape)


def split_halves(field):
    return jnp.concatenate([field[:, :OWN], field[:, OWN:]], axis=0)


def gather_body(recv_ref, msg_ref):
    total = jnp.sum(recv_ref[...], axis=0, keepdims=True)
    msg_ref[...] = jnp.broadcast_to(total, msg_ref.shape)


def end_body(rows_ref, applied_ref, corr_ref, sol_ref, mine_ref, sol_out, res_out):
    damping = by_half(damping_of(rows_ref[...]))
    sol_out[...] = split_halves(sol_ref[...] + damping * corr_ref[...])
    res_out[...] = split_halves(mine_ref[...] - damping * applied_ref[...])


def call(body, outs, *args, scratch=(), spaces=None, flops=1 << 20, name):
    return pl.pallas_call(
        body,
        out_shape=[jax.ShapeDtypeStruct(s, d) for s, d in outs],
        in_specs=[
            pl.BlockSpec(memory_space=s) for s in spaces or (pltpu.VMEM,) * len(args)
        ],
        out_specs=[pl.BlockSpec(memory_space=pltpu.VMEM)] * len(outs),
        scratch_shapes=list(scratch),
        compiler_params=PARAMS,
        cost_estimate=pl.CostEstimate(flops=flops, transcendentals=0, bytes_accessed=1 << 20),
        name=name,
    )(*args)


def stay(array):
    return pltpu.with_memory_space_constraint(array, pltpu.HBM)


def swap(array, axis):
    return lax.all_to_all(array, axis, split_axis=0, concat_axis=0, tiled=True)


def body(features, targets, point_order, lengthscale, noise_var):
    packed = (RHS // 2, 2 * OWN)
    n_p = N_X * N_C
    plane_msg, feat_msg = call(
        pack_body,
        [((n_p * SENT, 128), F32), ((N_Z, 8, 128), F32)],
        *map(stay, (features, targets, point_order[None, :], lengthscale)),
        scratch=[
            pltpu.VMEM((FEATS, OWN), F32),
            pltpu.VMEM((RHS, OWN), F32),
            pltpu.VMEM((1, OWN), jnp.int32),
            pltpu.SMEM((FEATS,), F32),
            pltpu.SemaphoreType.DMA((4,)),
        ],
        spaces=(pltpu.HBM,) * 4,
        name="pack",
    )
    plane = swap(plane_msg.reshape(n_p, 1, SENT * 128), PLANE).reshape(n_p * SENT, 128)
    feat = swap(feat_msg, Z)
    blocks, state, left = call(
        first_body,
        [
            ((N_X, BLOCK, BLOCK), BF16),
            ((2 * RHS, FLAT + 128), F32),
            ((FLAT, DEPTH), BF16),
        ],
        plane,
        stay(noise_var),
        scratch=[pltpu.SMEM((RHS,), F32), pltpu.SemaphoreType.DMA],
        spaces=(pltpu.VMEM, pltpu.HBM),
        flops=1 << 31,
        name="first",
    )
    line_msg, kern = call(
        build_body,
        [((N_Z, *packed), F32), ((FLAT, LINE), BF16)],
        feat,
        left,
        state,
        name="build",
    )
    line = swap(line_msg, Z)
    (share_msg,) = call(
        share_body, [((n_p, *packed), F32)], line, state, name="share"
    )
    shared = swap(share_msg, PLANE)
    sums_msg, applied = call(
        sums_body, [((N_Z, 128), F32), ((RHS, FLAT), F32)], shared, state, name="sums"
    )
    sums = swap(sums_msg, Z)
    line_msg, corr_2, sol, mine = call(
        second_body,
        [((N_Z, *packed), F32), (packed, F32), (packed, F32), (packed, F32)],
        sums,
        applied,
        state,
        blocks,
        kern,
        shared,
        name="second",
    )
    line = swap(line_msg, Z)
    near_msg, applied = call(
        last_sums_body,
        [((n_p, 128), F32), (packed, F32)],
        line,
        corr_2,
        state,
        mine,
        name="last_sums",
    )
    near = swap(near_msg, PLANE)
    (sums_msg,) = call(gather_body, [((N_Z, 128), F32)], near, name="near")
    sums = swap(sums_msg, Z)
    return tuple(
        call(
            end_body,
            [((RHS, OWN), F32)] * 2,
            sums,
            applied,
            corr_2,
            sol,
            mine,
            name="end",
        )
    )


def solution(mesh):
    finer = Mesh(mesh.devices.reshape(N_X, N_Z, 4, 2), ROWS_COLS)
    in_specs = (P(None, ROWS_COLS), P(None, ROWS_COLS), P(ROWS_COLS), P(), P())
    out_specs = (P(None, ROWS_COLS), P(None, ROWS_COLS))
    return jax.shard_map(body, mesh=finer, in_specs=in_specs, out_specs=out_specs, check_vma=False)
```

```python
import jax
import jax.numpy as jnp
from jax import lax
from jax.experimental import pallas as pl
from jax.experimental.pallas import tpu as pltpu
from jax.sharding import Mesh
from jax.sharding import PartitionSpec as P

INNER = 3
X, Z, Y, K = "rows_0", "rows_1", "cols_0", "cols_1"
PLANE = (X, Y, K)
ROWS_COLS = (X, Z, Y, K)
N_X, N_Z, N_C = 4, 16, 8
FEATS, RHS, OWN, BLOCK = 16, 32, 64, 512
LINE, FLAT = N_Z * OWN, N_X * BLOCK
DEPTH = 7 * FEATS
SENT = FEATS // 2 + RHS // 2 + 1
ROOT_LOG2E = 1.4426950408889634**0.5
F32, BF16 = jnp.float32, jnp.bfloat16
PARAMS = pltpu.CompilerParams(vmem_limit_bytes=12 * 1024 * 1024)


def low_lanes(rows):
    return lax.broadcasted_iota(jnp.int32, (rows, 2 * OWN), 1) < OWN


def join(a, b):
    low = low_lanes(a.shape[0])
    top = jnp.where(low, a, pltpu.roll(b, OWN, 1))
    bottom = jnp.where(low, pltpu.roll(a, OWN, 1), b)
    return jnp.concatenate([top, bottom], axis=0)


def part(field):
    half = field.shape[0] // 2
    top, bottom = field[:half], field[half:]
    low = low_lanes(half)
    return (
        jnp.where(low, top, pltpu.roll(bottom, OWN, 1)),
        jnp.where(low, pltpu.roll(top, OWN, 1), bottom),
    )


def join_all(pieces):
    tiles = [join(a, b) for a, b in zip(pieces[0::2], pieces[1::2])]
    return jnp.concatenate(tiles, axis=1)


def part_all(field):
    pieces = []
    for at in range(0, field.shape[1], 2 * OWN):
        pieces += part(field[:, at : at + 2 * OWN])
    return pieces


def own_piece(pieces):
    me = lax.axis_index(PLANE)
    mine = jnp.zeros_like(pieces[0])
    for which, piece in enumerate(pieces):
        mine = jnp.where(me == which, piece, mine)
    return mine


def by_half(column):
    half = column.shape[0] // 2
    return jnp.where(low_lanes(half), column[:half], column[half:])


def three(value):
    first = value.astype(BF16).astype(F32)
    second = (value - first).astype(BF16).astype(F32)
    third = (value - first - second).astype(BF16).astype(F32)
    return first, second, third


def factors(parts, side):
    p1, p2, p3 = parts
    scaled = p1 + (p2 + p3)
    h1, h2, h3 = three(-0.5 * jnp.sum(scaled * scaled, axis=0, keepdims=True))
    row = lax.broadcasted_iota(jnp.int32, scaled.shape, 0)
    at = 0 if side == 0 else 3
    tail = jnp.where(row < 6, 1.0, 0.0)
    for offset, h in enumerate((h1, h2, h3)):
        tail = jnp.where(row == at + offset, h, tail)
    order = (p1, p1, p2, p2, p1, p3) if side == 0 else (p1, p2, p1, p2, p3, p1)
    return jnp.concatenate([*order, tail], axis=0).astype(BF16)


def plane_cg(residual, kern_ref, noise):
    def stack(field):
        return jnp.concatenate([cut(field, x) for x in range(N_X)], axis=0)

    def image_of(direction):
        packed = direction.astype(BF16)
        images = [
            jnp.dot(
                packed[x * RHS : (x + 1) * RHS], kern_ref[x], preferred_element_type=F32
            )
            for x in range(N_X)
        ]
        return jnp.concatenate(images, axis=0) + shift * direction

    shift = jnp.concatenate([noise] * N_X, axis=0)
    remains = direction = stack(residual)
    correction = jnp.zeros_like(remains)
    res_norm = jnp.sum(remains * remains, axis=1, keepdims=True)
    for turn in range(INNER):
        image = image_of(direction)
        step = res_norm / jnp.sum(direction * image, axis=1, keepdims=True)
        correction = correction + step * direction
        if turn + 1 < INNER:
            remains = remains - step * image
            new_norm = jnp.sum(remains * remains, axis=1, keepdims=True)
            direction = remains + (new_norm / res_norm) * direction
            res_norm = new_norm
    pieces = [correction[x * RHS : (x + 1) * RHS] for x in range(N_X)]
    return jnp.concatenate(pieces, axis=1)


def sums_row(residual, applied):
    lane = lax.broadcasted_iota(jnp.int32, (RHS, 128), 1)
    cross = jnp.sum(residual * applied, axis=1, keepdims=True)
    energy = jnp.sum(applied * applied, axis=1, keepdims=True)
    turned = jnp.where(lane == 0, cross, jnp.where(lane == 1, energy, 0.0)).T
    blank = jnp.zeros((1, 128 - 2 * RHS), F32)
    return jnp.concatenate([turned[0:1], turned[1:2], blank], axis=1)


def damping_of(rows):
    total = jnp.sum(rows, axis=0, keepdims=True)
    turned = jnp.broadcast_to(total, (8, 128)).T
    return turned[0:RHS, 0:1] / (turned[RHS : 2 * RHS, 0:1] + 1e-6)


def column(source, shape):
    row = lax.broadcasted_iota(jnp.int32, shape, 0)
    filled = jnp.zeros(shape, F32)
    for i in range(shape[0]):
        filled = jnp.where(row == i, source[i], filled)
    return filled


SIDE = pl.ds(FLAT, 128)


def noise_of(state_ref):
    return state_ref[0:RHS, FLAT : FLAT + 1]


def own_correction(state_ref):
    return state_ref[RHS : RHS + RHS // 2, SIDE]


def own_residual(state_ref):
    return state_ref[RHS + RHS // 2 :, SIDE]


def pack_body(
    feat_any, targ_any, order_any, scale_any,
    plane_ref, line_ref,
    feat_ref, targ_ref, order_ref, scale_ref, sems,
):
    pairs = (
        (scale_any, scale_ref),
        (feat_any, feat_ref),
        (targ_any, targ_ref),
        (order_any, order_ref),
    )
    copies = [
        pltpu.make_async_copy(src, dst, sems.at[i]) for i, (src, dst) in enumerate(pairs)
    ]
    for copy in copies:
        copy.start()
    for copy in copies:
        copy.wait()

    def halves(field):
        half = field.shape[0] // 2
        return jnp.concatenate([field[:half], field[half:]], axis=1)

    scaled = halves(feat_ref[...] / column(scale_ref, (FEATS, OWN)) * ROOT_LOG2E)
    order = (order_ref[...] % BLOCK).astype(F32)
    order = jnp.concatenate([order, order], axis=1)
    whole = jnp.concatenate([scaled, halves(targ_ref[...]), order], axis=0)
    for to in range(N_X * N_C):
        plane_ref[pl.ds(SENT * to, SENT), :] = whole
    for to in range(N_Z):
        line_ref[to] = scaled


def cut(field, which):
    return field[:, which * BLOCK : (which + 1) * BLOCK]


def first_body(recv_ref, noise_any, kern_ref, state_ref, left_ref, given_ref, sem):
    copy = pltpu.make_async_copy(noise_any, given_ref, sem)
    copy.start()
    for x in range(N_X):
        at = x * N_C * SENT
        pieces = [recv_ref[pl.ds(at + i * SENT, SENT), :] for i in range(N_C)]
        parts = three(join_all([p[0:8] for p in pieces]))
        left = factors(parts, 0).T
        left_ref[pl.ds(x * BLOCK, BLOCK), :] = left
        exponent = jnp.dot(left, factors(parts, 1), preferred_element_type=F32)
        kern_ref[x] = jnp.exp2(exponent).astype(BF16)
        low = low_lanes(1)
        order = [
            jnp.where(low, a[24:25], b[24:25])
            for a, b in zip(pieces[0::2], pieces[1::2])
        ]
        order = jnp.concatenate(order, axis=1).astype(jnp.int32)
        index = lax.broadcasted_iota(jnp.int32, (BLOCK, BLOCK), 0)
        pick = jnp.where(index == order, 1.0, 0.0).astype(BF16)
        targets = three(join_all([p[8:24] for p in pieces]))
        stack = jnp.concatenate(targets, axis=0).astype(BF16)
        moved = jnp.dot(stack, pick, preferred_element_type=F32)
        residual = moved[0:RHS] + (moved[RHS : 2 * RHS] + moved[2 * RHS :])
        state_ref[0:RHS, pl.ds(x * BLOCK, BLOCK)] = residual
    copy.wait()
    noise = column(given_ref, (RHS, 128))
    state_ref[0:RHS, SIDE] = noise
    residual = state_ref[0:RHS, 0:FLAT]
    correction = plane_cg(residual, kern_ref, noise[:, 0:1])
    state_ref[RHS:, 0:FLAT] = correction
    both = [own_piece(part_all(field)) for field in (correction, residual)]
    state_ref[RHS:, SIDE] = jnp.concatenate(both, axis=0)


def spread(msg_ref, at, field):
    for which, piece in enumerate(part_all(field)):
        msg_ref[at + which] = piece


TILE = min(LINE, 256)


def build_body(line_ref, left_ref, state_ref, msg_ref, kern_ref):
    def piece(i):
        return line_ref[i]

    packed = state_ref[RHS:, 0:FLAT].astype(BF16)
    for at in range(0, LINE, TILE):
        tiles = range(at // OWN, (at + TILE) // OWN, 2)
        field = jnp.concatenate([join(piece(i), piece(i + 1)) for i in tiles], axis=1)
        exponent = jnp.dot(
            left_ref[...], factors(three(field), 1), preferred_element_type=F32
        )
        kern = jnp.exp2(exponent).astype(BF16)
        kern_ref[:, pl.ds(at, TILE)] = kern
        moved = jnp.dot(packed, kern, preferred_element_type=F32)
        spread(msg_ref, at // OWN, moved)


def applied_of(recv_ref, correction, state_ref):
    total = recv_ref[0]
    for i in range(1, recv_ref.shape[0]):
        total = total + recv_ref[i]
    return total + by_half(noise_of(state_ref)) * correction


def share_body(recv_ref, state_ref, msg_ref):
    applied = applied_of(recv_ref, own_correction(state_ref), state_ref)
    for to in range(N_X * N_C):
        msg_ref[to] = applied


def sums_body(recv_ref, state_ref, msg_ref, applied_ref):
    applied = join_all([recv_ref[i] for i in range(N_X * N_C)])
    applied_ref[...] = applied
    row = sums_row(state_ref[0:RHS, 0:FLAT], applied)
    msg_ref[...] = jnp.broadcast_to(row, msg_ref.shape)


def second_body(
    rows_ref, applied_ref, state_ref, block_ref, kern_ref, near_ref,
    msg_ref, new_ref, sol_ref, mine_ref,
):
    damping = damping_of(rows_ref[...])
    residual = state_ref[0:RHS, 0:FLAT] - damping * applied_ref[...]
    correction = plane_cg(residual, block_ref, noise_of(state_ref))
    packed = correction.astype(BF16)
    for at in range(0, LINE, TILE):
        moved = jnp.dot(packed, kern_ref[:, pl.ds(at, TILE)], preferred_element_type=F32)
        spread(msg_ref, at // OWN, moved)
    new_ref[...] = own_piece(part_all(correction))
    sol_ref[...] = by_half(damping) * own_correction(state_ref)
    mine = own_piece([near_ref[i] for i in range(N_X * N_C)])
    mine_ref[...] = own_residual(state_ref) - by_half(damping) * mine


def last_sums_body(recv_ref, corr_ref, state_ref, mine_ref, msg_ref, applied_ref):
    applied = applied_of(recv_ref, corr_ref[...], state_ref)
    applied_ref[...] = applied
    row = sums_row(split_halves(mine_ref[...]), split_halves(applied))
    msg_ref[...] = jnp.broadcast_to(row, msg_ref.shape)


def split_halves(field):
    return jnp.concatenate([field[:, :OWN], field[:, OWN:]], axis=0)


def gather_body(recv_ref, msg_ref):
    total = jnp.sum(recv_ref[...], axis=0, keepdims=True)
    msg_ref[...] = jnp.broadcast_to(total, msg_ref.shape)


def end_body(rows_ref, applied_ref, corr_ref, sol_ref, mine_ref, sol_out, res_out):
    damping = by_half(damping_of(rows_ref[...]))
    sol_out[...] = split_halves(sol_ref[...] + damping * corr_ref[...])
    res_out[...] = split_halves(mine_ref[...] - damping * applied_ref[...])


def call(body, outs, *args, scratch=(), spaces=None, flops=1 << 20, name):
    return pl.pallas_call(
        body,
        out_shape=[jax.ShapeDtypeStruct(s, d) for s, d in outs],
        in_specs=[
            pl.BlockSpec(memory_space=s) for s in spaces or (pltpu.VMEM,) * len(args)
        ],
        out_specs=[pl.BlockSpec(memory_space=pltpu.VMEM)] * len(outs),
        scratch_shapes=list(scratch),
        compiler_params=PARAMS,
        cost_estimate=pl.CostEstimate(flops=flops, transcendentals=0, bytes_accessed=1 << 20),
        name=name,
    )(*args)


def stay(array):
    return pltpu.with_memory_space_constraint(array, pltpu.HBM)


def swap(array, axis):
    return lax.all_to_all(array, axis, split_axis=0, concat_axis=0, tiled=True)


def body(features, targets, point_order, lengthscale, noise_var):
    packed = (RHS // 2, 2 * OWN)
    n_p = N_X * N_C
    plane_msg, feat_msg = call(
        pack_body,
        [((n_p * SENT, 128), F32), ((N_Z, 8, 128), F32)],
        *map(stay, (features, targets, point_order[None, :], lengthscale)),
        scratch=[
            pltpu.VMEM((FEATS, OWN), F32),
            pltpu.VMEM((RHS, OWN), F32),
            pltpu.VMEM((1, OWN), jnp.int32),
            pltpu.SMEM((FEATS,), F32),
            pltpu.SemaphoreType.DMA((4,)),
        ],
        spaces=(pltpu.HBM,) * 4,
        name="pack",
    )
    plane = swap(plane_msg.reshape(n_p, 1, SENT * 128), PLANE).reshape(n_p * SENT, 128)
    feat = swap(feat_msg, Z)
    blocks, state, left = call(
        first_body,
        [
            ((N_X, BLOCK, BLOCK), BF16),
            ((2 * RHS, FLAT + 128), F32),
            ((FLAT, DEPTH), BF16),
        ],
        plane,
        stay(noise_var),
        scratch=[pltpu.SMEM((RHS,), F32), pltpu.SemaphoreType.DMA],
        spaces=(pltpu.VMEM, pltpu.HBM),
        flops=1 << 31,
        name="first",
    )
    line_msg, kern = call(
        build_body,
        [((N_Z, *packed), F32), ((FLAT, LINE), BF16)],
        feat,
        left,
        state,
        name="build",
    )
    line = swap(line_msg, Z)
    (share_msg,) = call(
        share_body, [((n_p, *packed), F32)], line, state, name="share"
    )
    shared = swap(share_msg, PLANE)
    sums_msg, applied = call(
        sums_body, [((N_Z, 128), F32), ((RHS, FLAT), F32)], shared, state, name="sums"
    )
    sums = swap(sums_msg, Z)
    line_msg, corr_2, sol, mine = call(
        second_body,
        [((N_Z, *packed), F32), (packed, F32), (packed, F32), (packed, F32)],
        sums,
        applied,
        state,
        blocks,
        kern,
        shared,
        name="second",
    )
    line = swap(line_msg, Z)
    near_msg, applied = call(
        last_sums_body,
        [((n_p // 2, 128), F32), (packed, F32)],
        line,
        corr_2,
        state,
        mine,
        name="last_sums",
    )
    near = swap(near_msg, (X, Y))
    (sums_msg,) = call(gather_body, [((2 * N_Z, 128), F32)], near, name="near")
    sums = swap(sums_msg, (Z, K))
    return tuple(
        call(
            end_body,
            [((RHS, OWN), F32)] * 2,
            sums,
            applied,
            corr_2,
            sol,
            mine,
            name="end",
        )
    )


def solution(mesh):
    finer = Mesh(mesh.devices.reshape(N_X, N_Z, 4, 2), ROWS_COLS)
    in_specs = (P(None, ROWS_COLS), P(None, ROWS_COLS), P(ROWS_COLS), P(), P())
    out_specs = (P(None, ROWS_COLS), P(None, ROWS_COLS))
    return jax.shard_map(body, mesh=finer, in_specs=in_specs, out_specs=out_specs, check_vma=False)
```

```python
import jax
import jax.numpy as jnp
from jax import lax
from jax.experimental import pallas as pl
from jax.experimental.pallas import tpu as pltpu
from jax.sharding import Mesh
from jax.sharding import PartitionSpec as P

INNER = 3
X, Z, Y, K = "rows_0", "rows_1", "cols_0", "cols_1"
PLANE = (X, Y, K)
ROWS_COLS = (X, Z, Y, K)
N_X, N_Z, N_C = 4, 16, 8
FEATS, RHS, OWN, BLOCK = 16, 32, 64, 512
LINE, FLAT = N_Z * OWN, N_X * BLOCK
DEPTH = 7 * FEATS
SENT = FEATS // 2 + RHS // 2 + 1
ROOT_LOG2E = 1.4426950408889634**0.5
F32, BF16 = jnp.float32, jnp.bfloat16
PARAMS = pltpu.CompilerParams(vmem_limit_bytes=12 * 1024 * 1024)


def low_lanes(rows):
    return lax.broadcasted_iota(jnp.int32, (rows, 2 * OWN), 1) < OWN


def join(a, b):
    low = low_lanes(a.shape[0])
    top = jnp.where(low, a, pltpu.roll(b, OWN, 1))
    bottom = jnp.where(low, pltpu.roll(a, OWN, 1), b)
    return jnp.concatenate([top, bottom], axis=0)


def part(field):
    half = field.shape[0] // 2
    top, bottom = field[:half], field[half:]
    low = low_lanes(half)
    return (
        jnp.where(low, top, pltpu.roll(bottom, OWN, 1)),
        jnp.where(low, pltpu.roll(top, OWN, 1), bottom),
    )


def join_all(pieces):
    tiles = [join(a, b) for a, b in zip(pieces[0::2], pieces[1::2])]
    return jnp.concatenate(tiles, axis=1)


def part_all(field):
    pieces = []
    for at in range(0, field.shape[1], 2 * OWN):
        pieces += part(field[:, at : at + 2 * OWN])
    return pieces


def own_piece(pieces):
    me = lax.axis_index(PLANE)
    mine = jnp.zeros_like(pieces[0])
    for which, piece in enumerate(pieces):
        mine = jnp.where(me == which, piece, mine)
    return mine


def by_half(column):
    half = column.shape[0] // 2
    return jnp.where(low_lanes(half), column[:half], column[half:])


def three(value):
    first = value.astype(BF16).astype(F32)
    second = (value - first).astype(BF16).astype(F32)
    third = (value - first - second).astype(BF16).astype(F32)
    return first, second, third


def factors(parts, side):
    p1, p2, p3 = parts
    scaled = p1 + (p2 + p3)
    h1, h2, h3 = three(-0.5 * jnp.sum(scaled * scaled, axis=0, keepdims=True))
    row = lax.broadcasted_iota(jnp.int32, scaled.shape, 0)
    at = 0 if side == 0 else 3
    tail = jnp.where(row < 6, 1.0, 0.0)
    for offset, h in enumerate((h1, h2, h3)):
        tail = jnp.where(row == at + offset, h, tail)
    order = (p1, p1, p2, p2, p1, p3) if side == 0 else (p1, p2, p1, p2, p3, p1)
    return jnp.concatenate([*order, tail], axis=0).astype(BF16)


def plane_cg(residual, kern_ref, noise):
    def stack(field):
        return jnp.concatenate([cut(field, x) for x in range(N_X)], axis=0)

    def image_of(direction):
        packed = direction.astype(BF16)
        images = [
            jnp.dot(
                packed[x * RHS : (x + 1) * RHS], kern_ref[x], preferred_element_type=F32
            )
            for x in range(N_X)
        ]
        return jnp.concatenate(images, axis=0) + shift * direction

    shift = jnp.concatenate([noise] * N_X, axis=0)
    remains = direction = stack(residual)
    correction = jnp.zeros_like(remains)
    res_norm = jnp.sum(remains * remains, axis=1, keepdims=True)
    for turn in range(INNER):
        image = image_of(direction)
        step = res_norm / jnp.sum(direction * image, axis=1, keepdims=True)
        correction = correction + step * direction
        if turn + 1 < INNER:
            remains = remains - step * image
            new_norm = jnp.sum(remains * remains, axis=1, keepdims=True)
            direction = remains + (new_norm / res_norm) * direction
            res_norm = new_norm
    pieces = [correction[x * RHS : (x + 1) * RHS] for x in range(N_X)]
    return jnp.concatenate(pieces, axis=1)


def sums_row(residual, applied):
    lane = lax.broadcasted_iota(jnp.int32, (RHS, 128), 1)
    cross = jnp.sum(residual * applied, axis=1, keepdims=True)
    energy = jnp.sum(applied * applied, axis=1, keepdims=True)
    turned = jnp.where(lane == 0, cross, jnp.where(lane == 1, energy, 0.0)).T
    blank = jnp.zeros((1, 128 - 2 * RHS), F32)
    return jnp.concatenate([turned[0:1], turned[1:2], blank], axis=1)


def damping_of(rows):
    total = jnp.sum(rows, axis=0, keepdims=True)
    turned = jnp.broadcast_to(total, (8, 128)).T
    return turned[0:RHS, 0:1] / (turned[RHS : 2 * RHS, 0:1] + 1e-6)


def column(source, shape):
    row = lax.broadcasted_iota(jnp.int32, shape, 0)
    filled = jnp.zeros(shape, F32)
    for i in range(shape[0]):
        filled = jnp.where(row == i, source[i], filled)
    return filled


SIDE = pl.ds(FLAT, 128)


def noise_of(state_ref):
    return state_ref[0:RHS, FLAT : FLAT + 1]


def own_correction(state_ref):
    return state_ref[RHS : RHS + RHS // 2, SIDE]


def own_residual(state_ref):
    return state_ref[RHS + RHS // 2 :, SIDE]


def pack_body(
    feat_any, targ_any, order_any, scale_any,
    plane_ref, line_ref,
    feat_ref, targ_ref, order_ref, scale_ref, copies_ref, sems,
):
    pairs = (
        (scale_any, scale_ref),
        (feat_any, feat_ref),
        (targ_any, targ_ref),
        (order_any, order_ref),
    )
    copies = [
        pltpu.make_async_copy(src, dst, sems.at[i]) for i, (src, dst) in enumerate(pairs)
    ]
    for copy in copies:
        copy.start()

    def halves(field):
        half = field.shape[0] // 2
        return jnp.concatenate([field[:half], field[half:]], axis=1)

    copies[0].wait()
    copies[1].wait()
    scaled = halves(feat_ref[...] / column(scale_ref, (FEATS, OWN)) * ROOT_LOG2E)
    for to in range(N_Z):
        copies_ref[to] = scaled
    out = pltpu.make_async_copy(copies_ref, line_ref, sems.at[4])
    out.start()
    copies[2].wait()
    copies[3].wait()
    order = (order_ref[...] % BLOCK).astype(F32)
    order = jnp.concatenate([order, order], axis=1)
    whole = jnp.concatenate([scaled, halves(targ_ref[...]), order], axis=0)
    for to in range(N_X * N_C):
        plane_ref[pl.ds(SENT * to, SENT), :] = whole
    out.wait()


def cut(field, which):
    return field[:, which * BLOCK : (which + 1) * BLOCK]


def first_body(recv_ref, noise_any, kern_ref, state_ref, left_ref, given_ref, sem):
    copy = pltpu.make_async_copy(noise_any, given_ref, sem)
    copy.start()
    for x in range(N_X):
        at = x * N_C * SENT
        pieces = [recv_ref[pl.ds(at + i * SENT, SENT), :] for i in range(N_C)]
        parts = three(join_all([p[0:8] for p in pieces]))
        left = factors(parts, 0).T
        left_ref[pl.ds(x * BLOCK, BLOCK), :] = left
        exponent = jnp.dot(left, factors(parts, 1), preferred_element_type=F32)
        kern_ref[x] = jnp.exp2(exponent).astype(BF16)
        low = low_lanes(1)
        order = [
            jnp.where(low, a[24:25], b[24:25])
            for a, b in zip(pieces[0::2], pieces[1::2])
        ]
        order = jnp.concatenate(order, axis=1).astype(jnp.int32)
        index = lax.broadcasted_iota(jnp.int32, (BLOCK, BLOCK), 0)
        pick = jnp.where(index == order, 1.0, 0.0).astype(BF16)
        targets = three(join_all([p[8:24] for p in pieces]))
        stack = jnp.concatenate(targets, axis=0).astype(BF16)
        moved = jnp.dot(stack, pick, preferred_element_type=F32)
        residual = moved[0:RHS] + (moved[RHS : 2 * RHS] + moved[2 * RHS :])
        state_ref[0:RHS, pl.ds(x * BLOCK, BLOCK)] = residual
    copy.wait()
    noise = column(given_ref, (RHS, 128))
    state_ref[0:RHS, SIDE] = noise
    residual = state_ref[0:RHS, 0:FLAT]
    correction = plane_cg(residual, kern_ref, noise[:, 0:1])
    state_ref[RHS:, 0:FLAT] = correction
    both = [own_piece(part_all(field)) for field in (correction, residual)]
    state_ref[RHS:, SIDE] = jnp.concatenate(both, axis=0)


def spread(msg_ref, at, field):
    for which, piece in enumerate(part_all(field)):
        msg_ref[at + which] = piece


TILE = min(LINE, 256)


def build_body(line_ref, left_ref, state_ref, msg_ref, kern_ref):
    def piece(i):
        return line_ref[i]

    packed = state_ref[RHS:, 0:FLAT].astype(BF16)
    for at in range(0, LINE, TILE):
        tiles = range(at // OWN, (at + TILE) // OWN, 2)
        field = jnp.concatenate([join(piece(i), piece(i + 1)) for i in tiles], axis=1)
        exponent = jnp.dot(
            left_ref[...], factors(three(field), 1), preferred_element_type=F32
        )
        kern = jnp.exp2(exponent).astype(BF16)
        kern_ref[:, pl.ds(at, TILE)] = kern
        moved = jnp.dot(packed, kern, preferred_element_type=F32)
        spread(msg_ref, at // OWN, moved)


def applied_of(recv_ref, correction, state_ref):
    total = recv_ref[0]
    for i in range(1, recv_ref.shape[0]):
        total = total + recv_ref[i]
    return total + by_half(noise_of(state_ref)) * correction


def share_body(recv_ref, state_ref, msg_ref):
    applied = applied_of(recv_ref, own_correction(state_ref), state_ref)
    for to in range(N_X * N_C):
        msg_ref[to] = applied


def sums_body(recv_ref, state_ref, msg_ref, applied_ref):
    applied = join_all([recv_ref[i] for i in range(N_X * N_C)])
    applied_ref[...] = applied
    row = sums_row(state_ref[0:RHS, 0:FLAT], applied)
    msg_ref[...] = jnp.broadcast_to(row, msg_ref.shape)


def second_body(
    rows_ref, applied_ref, state_ref, block_ref, kern_ref, near_ref,
    msg_ref, new_ref, sol_ref, mine_ref,
):
    damping = damping_of(rows_ref[...])
    residual = state_ref[0:RHS, 0:FLAT] - damping * applied_ref[...]
    correction = plane_cg(residual, block_ref, noise_of(state_ref))
    packed = correction.astype(BF16)
    for at in range(0, LINE, TILE):
        moved = jnp.dot(packed, kern_ref[:, pl.ds(at, TILE)], preferred_element_type=F32)
        spread(msg_ref, at // OWN, moved)
    new_ref[...] = own_piece(part_all(correction))
    sol_ref[...] = by_half(damping) * own_correction(state_ref)
    mine = own_piece([near_ref[i] for i in range(N_X * N_C)])
    mine_ref[...] = own_residual(state_ref) - by_half(damping) * mine


def last_sums_body(recv_ref, corr_ref, state_ref, mine_ref, msg_ref, applied_ref):
    applied = applied_of(recv_ref, corr_ref[...], state_ref)
    applied_ref[...] = applied
    row = sums_row(split_halves(mine_ref[...]), split_halves(applied))
    msg_ref[...] = jnp.broadcast_to(row, msg_ref.shape)


def split_halves(field):
    return jnp.concatenate([field[:, :OWN], field[:, OWN:]], axis=0)


def gather_body(recv_ref, msg_ref):
    total = jnp.sum(recv_ref[...], axis=0, keepdims=True)
    msg_ref[...] = jnp.broadcast_to(total, msg_ref.shape)


def end_body(rows_ref, applied_ref, corr_ref, sol_ref, mine_ref, sol_out, res_out):
    damping = by_half(damping_of(rows_ref[...]))
    sol_out[...] = split_halves(sol_ref[...] + damping * corr_ref[...])
    res_out[...] = split_halves(mine_ref[...] - damping * applied_ref[...])


def call(body, outs, *args, scratch=(), spaces=None, out_spaces=None, flops=1 << 20, name):
    return pl.pallas_call(
        body,
        out_shape=[jax.ShapeDtypeStruct(s, d) for s, d in outs],
        in_specs=[
            pl.BlockSpec(memory_space=s) for s in spaces or (pltpu.VMEM,) * len(args)
        ],
        out_specs=[
            pl.BlockSpec(memory_space=s) for s in out_spaces or (pltpu.VMEM,) * len(outs)
        ],
        scratch_shapes=list(scratch),
        compiler_params=PARAMS,
        cost_estimate=pl.CostEstimate(flops=flops, transcendentals=0, bytes_accessed=1 << 20),
        name=name,
    )(*args)


def stay(array):
    return pltpu.with_memory_space_constraint(array, pltpu.HBM)


def swap(array, axis):
    return lax.all_to_all(array, axis, split_axis=0, concat_axis=0, tiled=True)


def body(features, targets, point_order, lengthscale, noise_var):
    packed = (RHS // 2, 2 * OWN)
    n_p = N_X * N_C
    plane_msg, feat_msg = call(
        pack_body,
        [((n_p * SENT, 128), F32), ((N_Z, 8, 128), F32)],
        *map(stay, (features, targets, point_order[None, :], lengthscale)),
        scratch=[
            pltpu.VMEM((FEATS, OWN), F32),
            pltpu.VMEM((RHS, OWN), F32),
            pltpu.VMEM((1, OWN), jnp.int32),
            pltpu.SMEM((FEATS,), F32),
            pltpu.VMEM((N_Z, FEATS // 2, 2 * OWN), F32),
            pltpu.SemaphoreType.DMA((5,)),
        ],
        spaces=(pltpu.HBM,) * 4,
        out_spaces=(pltpu.VMEM, pltpu.HBM),
        name="pack",
    )
    plane = swap(plane_msg.reshape(n_p, 1, SENT * 128), PLANE).reshape(n_p * SENT, 128)
    feat = swap(feat_msg, Z)
    blocks, state, left = call(
        first_body,
        [
            ((N_X, BLOCK, BLOCK), BF16),
            ((2 * RHS, FLAT + 128), F32),
            ((FLAT, DEPTH), BF16),
        ],
        plane,
        stay(noise_var),
        scratch=[pltpu.SMEM((RHS,), F32), pltpu.SemaphoreType.DMA],
        spaces=(pltpu.VMEM, pltpu.HBM),
        flops=1 << 31,
        name="first",
    )
    line_msg, kern = call(
        build_body,
        [((N_Z, *packed), F32), ((FLAT, LINE), BF16)],
        feat,
        left,
        state,
        name="build",
    )
    line = swap(line_msg, Z)
    (share_msg,) = call(
        share_body, [((n_p, *packed), F32)], line, state, name="share"
    )
    shared = swap(share_msg, PLANE)
    sums_msg, applied = call(
        sums_body, [((N_Z, 128), F32), ((RHS, FLAT), F32)], shared, state, name="sums"
    )
    sums = swap(sums_msg, Z)
    line_msg, corr_2, sol, mine = call(
        second_body,
        [((N_Z, *packed), F32), (packed, F32), (packed, F32), (packed, F32)],
        sums,
        applied,
        state,
        blocks,
        kern,
        shared,
        name="second",
    )
    line = swap(line_msg, Z)
    near_msg, applied = call(
        last_sums_body,
        [((n_p, 128), F32), (packed, F32)],
        line,
        corr_2,
        state,
        mine,
        name="last_sums",
    )
    near = swap(near_msg, PLANE)
    (sums_msg,) = call(gather_body, [((N_Z, 128), F32)], near, name="near")
    sums = swap(sums_msg, Z)
    return tuple(
        call(
            end_body,
            [((RHS, OWN), F32)] * 2,
            sums,
            applied,
            corr_2,
            sol,
            mine,
            name="end",
        )
    )


def solution(mesh):
    finer = Mesh(mesh.devices.reshape(N_X, N_Z, 4, 2), ROWS_COLS)
    in_specs = (P(None, ROWS_COLS), P(None, ROWS_COLS), P(ROWS_COLS), P(), P())
    out_specs = (P(None, ROWS_COLS), P(None, ROWS_COLS))
    return jax.shard_map(body, mesh=finer, in_specs=in_specs, out_specs=out_specs, check_vma=False)
```
